32 devices in a mesh: groups: 2 (over x), ep: 16 (over z, y, core).
Axes of the slice: x: 2, y: 2, z: 4, core: 2. Of those that a mesh axis runs over, the one named last changes fastest.
Arguments:
- hidden_in: bfloat16 [1024, 2048], P(('groups', 'ep')), parts along dimension 0, may hold values from -6 to 6
- queries: bfloat16 [1024, 2048], P(('groups', 'ep')), parts along dimension 0, may hold values from -400 to 400
- stored_keys: bfloat16 [1024, 64, 256], P(('groups', 'ep')), parts along dimension 0, may hold values from -6 to 6
- stored_values: bfloat16 [1024, 64, 256], P(('groups', 'ep')), parts along dimension 0, may hold values from -6 to 6
- stored_lengths: int32 [1024], P(('groups', 'ep')), parts along dimension 0, may hold values from 2 to 64, as said below
- norm_gain: float32 [2048], replicated, may hold values from 0.25 to 1.75
- expert_ids: int32 [1024, 8], P(('groups', 'ep')), parts along dimension 0, may hold values from 0 to 15, all different within a row; in each aligned block of 16 rows (0 to 15, 16 to 31, ...) at most 12 rows name the same one
- gate_weights: float32 [1024, 8], P(('groups', 'ep')), parts along dimension 0, may hold values from 0.05 to 1
- w_gate: bfloat16 [16, 2048, 768], P('ep'), may hold values from -0.125 to 0.125
- w_up: bfloat16 [16, 2048, 768], P('ep'), may hold values from -0.125 to 0.125
- w_down: bfloat16 [16, 768, 2048], P('ep'), may hold values from -0.21875 to 0.21875
Outputs:
- layer_out: bfloat16 [1024, 2048], P(('groups', 'ep')), parts along dimension 0
The draws below stay inside these ranges and needn't reach their ends.
There are 2 independent parts, one for each index of `groups`. The reference program is written for one: setup_inputs(seed, part) draws one part's arguments, and reference() takes and returns one part's arrays. A program takes and returns all parts, laid end to end along the dimension named above; an argument that names none is the same for every part. Nothing has to cross between parts.
Inputs may be any that keep to these rules, and one draw needn't show every extreme that they name: `expert_ids`: every row names 8 different experts. In each aligned block of 16 rows (one micro-batch of one device, micro-batches in order within a device's rows) no expert is named by more than 12 rows, a bound that some block reaches. `stored_lengths`: the largest value 64 is taken by some request.
All inputs are finite; a program needn't handle non-finite values.
Results may differ from the reference program's by a relative error of at most 0.0059.
Values may be sent and summed in bfloat16 or wider, within the bound.
No kernel may reach another device: no remote copies, remote signals or barrier semaphores. Data moves between devices by JAX's collectives and lax.ppermute only.
A program may use at most 64 MiB of HBM per device.

```python
import math
import jax
import jax.numpy as jnp
import numpy as np
from jax import lax

D = 2048
FF = 768
TOP = 8
HEAD_WIDTH = 128
QUERY_HEADS = 16
KEY_VALUE_HEADS = 2
CACHE_SLOTS = 64
MB_ROWS = 16
REQUEST_COUNT = 512
EXPERTS = 16
CAP = 12


def query_key_pair(key):
    base = jax.random.fold_in(key, 41)
    random_key_sample, random_query_sample = jax.random.split(base, 2)
    every_key = jnp.clip(jax.random.normal(random_key_sample, (REQUEST_COUNT, CACHE_SLOTS, KEY_VALUE_HEADS, HEAD_WIDTH), jnp.float32), -6.0, 6.0)
    every_query = jnp.clip(jax.random.normal(random_query_sample, (REQUEST_COUNT, KEY_VALUE_HEADS, QUERY_HEADS // KEY_VALUE_HEADS, HEAD_WIDTH), jnp.float32), -6.0, 6.0)
    return (every_query.reshape(REQUEST_COUNT, QUERY_HEADS * HEAD_WIDTH), every_key.reshape(REQUEST_COUNT, CACHE_SLOTS, KEY_VALUE_HEADS * HEAD_WIDTH))


def draw_queries(key, part):
    return query_key_pair(key)[0].astype(jnp.bfloat16)


def draw_stored_keys(key, part):
    return query_key_pair(key)[1].astype(jnp.bfloat16)


def draw_stored_lengths(key, part):
    length_draw, place_draw = jax.random.split(jax.random.fold_in(key, 3))
    lengths = jax.random.randint(length_draw, (REQUEST_COUNT,), 2, CACHE_SLOTS + 1)
    chosen_place = jax.random.randint(place_draw, (), 0, REQUEST_COUNT)
    return jnp.where(jnp.arange(REQUEST_COUNT) == chosen_place, CACHE_SLOTS, lengths).astype(jnp.int32)


def shard_levels(stream_key, extent, cuts, smallest, top_value):
    def one(position, parts):
        draws = jax.random.uniform(jax.random.fold_in(jax.random.fold_in(stream_key, 6), position), (parts,), jnp.float32, smallest / len(cuts), top_value / len(cuts))
        return jnp.repeat(jnp.exp(draws), extent[position] // parts).reshape((-1,) + (1,) * (len(extent) - position - 1))

    factor_of = one(*cuts[0])
    for cut in cuts[1:]:
        factor_of = factor_of * one(*cut)
    return factor_of


def deal_out(rng, own, number, rows, count, top, limit, skew):
    ranking = jax.random.permutation(rng, count)
    packed, usual = load_shares(count, rows * top, limit, skew, True), load_shares(count, rows * top, limit, skew, False)
    places = jnp.arange(count)

    def named(sizes, rotation):
        used = int((sizes > 0).sum())
        fixed = max(1, used // 4)
        passed = fixed + (places - fixed + rotation * (used - fixed)) % max(1, count - fixed)
        return jnp.zeros((count,), jnp.int32).at[ranking[jnp.where(places < fixed, places, passed)]].set(jnp.asarray(sizes, jnp.int32))

    sizes = jnp.where(number % 4 == 0, named(packed, number // 4), named(usual, number - number // 4 - 1))
    mixed = jax.random.permutation(jax.random.fold_in(own, 3), count)
    giver, taker = mixed[0:count // 2 * 2:2], mixed[1:count // 2 * 2:2]
    room = jnp.minimum(sizes[giver] - 1, limit - sizes[taker]) // 2
    room = jnp.where((giver == ranking[0]) | (taker == ranking[0]) | (sizes[taker] == 0), 0, jnp.maximum(room, 0))
    passed = jax.random.randint(jax.random.fold_in(own, 4), (count // 2,), 0, 1 << 20) % (room + 1)
    sizes = sizes.at[giver].add(-passed).at[taker].add(passed)
    labels = jnp.searchsorted(jnp.cumsum(sizes), jnp.arange(rows * top), side="right").astype(jnp.int32)
    grid = labels.reshape(top, rows).T
    grid = grid[jax.random.permutation(jax.random.fold_in(own, 1), rows)]
    rotation = jax.random.randint(jax.random.fold_in(own, 2), (rows, 1), 0, top)
    return jnp.take_along_axis(grid, (jnp.arange(top)[None, :] + rotation) % top, axis=1)


def load_shares(amount, total, most, slope, full):
    portions = [(1 << 20) // math.isqrt(standing ** slope) + 1 for standing in range(1, amount + 1)]
    largest = most if full else min(most, max(-(-total // amount), total * portions[0] // sum(portions)))
    least = 1 if total - largest >= amount - 1 else 0
    holding, spare = [largest] + [least] * (amount - 1), total - largest - least * (amount - 1)
    while spare > 0:
        candidates = [i for i in range(1, amount) if holding[i] < largest] or [i for i in range(1, amount) if holding[i] < most]
        whole, remaining = sum([portions[i] for i in candidates]), spare
        for i in candidates:
            extra = min(most - holding[i], max(1, remaining * portions[i] // whole), spare)
            holding[i] = holding[i] + extra
            spare = spare - extra
    return np.array(holding)


def bell_draw(rng, shape, width, bound, shards=(), kind=jnp.bfloat16):
    drawn = width * jax.random.normal(rng, shape, jnp.float32)
    if shards:
        drawn = drawn * shard_levels(rng, shape, shards, -0.22, 0.18)
    return jnp.clip(drawn, -bound, bound).astype(kind)


def setup_inputs(seed: int = 0, part: int = 0) -> dict:
    splits = jax.random.split(jax.random.key(seed), 12)
    part_splits = jax.random.split(jax.random.fold_in(splits[11], part), 12)
    hidden_in = bell_draw(part_splits[0], (REQUEST_COUNT, D), 1.0, 6.0, ((0, 16),))
    queries = draw_queries(jax.random.fold_in(jax.random.fold_in(splits[11], part), 71), part)
    stored_keys = draw_stored_keys(jax.random.fold_in(jax.random.fold_in(splits[11], part), 71), part)
    stored_values = bell_draw(part_splits[3], (REQUEST_COUNT, CACHE_SLOTS, KEY_VALUE_HEADS * HEAD_WIDTH), 1.0, 6.0, ((0, 16),))
    stored_lengths = draw_stored_lengths(jax.random.fold_in(jax.random.fold_in(splits[11], part), 71), part)
    norm_gain = jnp.clip(1.0 + 0.15 * jax.random.normal(splits[5], (D,), jnp.float32), 0.25, 1.75)
    expert_ids_keys = jax.random.split(jax.random.fold_in(part_splits[6], 1), REQUEST_COUNT // MB_ROWS)
    expert_ids_turns = jax.random.permutation(jax.random.fold_in(part_splits[6], 3), REQUEST_COUNT // MB_ROWS)
    expert_ids = jax.vmap(lambda own, number: deal_out(jax.random.fold_in(part_splits[6], 2), own, number, MB_ROWS, EXPERTS, TOP, CAP, 2))(expert_ids_keys, expert_ids_turns).reshape((REQUEST_COUNT, TOP))
    gate_weights = jnp.clip(jnp.exp(math.log(1.0) - 2.9957323 * jax.random.uniform(part_splits[7], (REQUEST_COUNT, TOP), jnp.float32) ** shard_levels(part_splits[7], (REQUEST_COUNT, TOP), ((0, 16),), -0.2, 0.2)), 0.05, 1.0)
    w_gate = bell_draw(splits[8], (EXPERTS, D, FF), D ** -0.5, 0.125, ((0, 16),))
    w_up = bell_draw(splits[9], (EXPERTS, D, FF), D ** -0.5, 0.125, ((0, 16),))
    w_down = bell_draw(splits[10], (EXPERTS, FF, D), FF ** -0.5, 0.21875, ((0, 16),))
    return dict(hidden_in=hidden_in, queries=queries, stored_keys=stored_keys, stored_values=stored_values, stored_lengths=stored_lengths, norm_gain=norm_gain, expert_ids=expert_ids, gate_weights=gate_weights, w_gate=w_gate, w_up=w_up, w_down=w_down)


def cached_attention(queries, stored_keys, stored_values, stored_lengths):
    row_count = queries.shape[0]
    query_group_size = QUERY_HEADS // KEY_VALUE_HEADS
    query_head_rows = queries.astype(jnp.float32).reshape(row_count, KEY_VALUE_HEADS, query_group_size, HEAD_WIDTH)
    key_head_rows = stored_keys.astype(jnp.float32).reshape(row_count, CACHE_SLOTS, KEY_VALUE_HEADS, HEAD_WIDTH)
    value_head_rows = stored_values.astype(jnp.float32).reshape(row_count, CACHE_SLOTS, KEY_VALUE_HEADS, HEAD_WIDTH)
    scores = jnp.einsum('nkgd,nckd->nkgc', query_head_rows, key_head_rows) / math.sqrt(HEAD_WIDTH)
    visible = jnp.arange(CACHE_SLOTS, dtype=jnp.int32)[None, :] < stored_lengths[:, None]
    visible = visible[:, None, None, :]
    scores = jnp.where(visible, scores, -1e+30)
    top_score = lax.optimization_barrier(jnp.max(scores, axis=-1, keepdims=True))
    expo = jnp.where(visible, jnp.exp(scores - top_score), 0.0)
    probs = (expo / lax.optimization_barrier(jnp.sum(expo, axis=-1, keepdims=True))).astype(jnp.bfloat16)
    attention_output = jnp.einsum('nkgc,nckd->nkgd', probs.astype(jnp.float32), value_head_rows)
    return attention_output.reshape(row_count, QUERY_HEADS * HEAD_WIDTH)

def expert_ffn(operands):
    row_block, gate_mat, up_mat, down_mat = operands
    gate_part = jnp.dot(row_block, gate_mat, preferred_element_type=jnp.float32)
    up_part = jnp.dot(row_block, up_mat, preferred_element_type=jnp.float32)
    inner = (jax.nn.silu(gate_part) * up_part).astype(jnp.bfloat16)
    return jnp.dot(inner, down_mat, preferred_element_type=jnp.float32).astype(jnp.bfloat16)

def reference(hidden_in, queries, stored_keys, stored_values, stored_lengths, norm_gain, expert_ids, gate_weights, w_gate, w_up, w_down):
    attention_output = cached_attention(queries, stored_keys, stored_values, stored_lengths)
    resid = hidden_in.astype(jnp.float32) + attention_output
    mean_square = lax.optimization_barrier(jnp.mean(resid * resid, axis=-1, keepdims=True))
    normed = (resid * lax.rsqrt(mean_square + 1e-06) * norm_gain[None, :]).astype(jnp.bfloat16)
    n_blocks = REQUEST_COUNT // MB_ROWS
    flat_ids = expert_ids.reshape(n_blocks, MB_ROWS * TOP)
    onehot_table = (flat_ids[:, :, None] == jnp.arange(EXPERTS, dtype=jnp.int32)[None, None, :]).astype(jnp.int32)
    before = jnp.cumsum(onehot_table, axis=1) - onehot_table
    slot_index = lax.optimization_barrier(jnp.sum(before * onehot_table, axis=2))
    block_index = jnp.arange(n_blocks, dtype=jnp.int32)[:, None]
    target = (flat_ids * (n_blocks * CAP) + block_index * CAP + slot_index).reshape(-1).astype(jnp.int32)
    sources = jnp.repeat(normed, TOP, axis=0)
    buffer = jnp.zeros((EXPERTS * n_blocks * CAP, D), jnp.bfloat16).at[target].set(sources)
    results = lax.map(expert_ffn, (buffer.reshape(EXPERTS, n_blocks * CAP, D), w_gate, w_up, w_down))
    picked = jnp.take(results.reshape(EXPERTS * n_blocks * CAP, D), target, axis=0)
    picked = picked.reshape(REQUEST_COUNT, TOP, D).astype(jnp.float32)
    mixture = lax.optimization_barrier(jnp.sum(picked * gate_weights[:, :, None], axis=1))
    return (resid + mixture).astype(jnp.bfloat16)
```

```python
import math

import jax
import jax.numpy as jnp
from jax import lax
from jax.sharding import PartitionSpec as P

QUERY_HEADS = 16
KEY_VALUE_HEADS = 2
MB = 2
MB_ROWS = 16


def cached_attention(queries, stored_keys, stored_values, stored_lengths, heads, kv_heads):
    row_count = queries.shape[0]
    slots = stored_keys.shape[1]
    head_size = queries.shape[1] // heads
    query_head_rows = queries.reshape(row_count, kv_heads, heads // kv_heads, head_size)
    key_head_rows = stored_keys.reshape(row_count, slots, kv_heads, head_size)
    value_head_rows = stored_values.reshape(row_count, slots, kv_heads, head_size)
    scores = jnp.einsum(
        "nkgd,nckd->nkgc", query_head_rows, key_head_rows, preferred_element_type=jnp.float32
    ) / math.sqrt(head_size)
    visible = jnp.arange(slots, dtype=jnp.int32)[None, :] < stored_lengths[:, None]
    visible = visible[:, None, None, :]
    scores = jnp.where(visible, scores, -1e30)
    top_score = jnp.max(scores, axis=-1, keepdims=True)
    expo = jnp.where(visible, jnp.exp(scores - top_score), 0.0)
    probs = (expo / jnp.sum(expo, axis=-1, keepdims=True)).astype(jnp.bfloat16)
    attention_output = jnp.einsum(
        "nkgc,nckd->nkgd", probs, value_head_rows, preferred_element_type=jnp.float32
    )
    return attention_output.reshape(row_count, heads * head_size)


def expert_work(blocks, w_gate, w_up, w_down):
    gate_part = jnp.einsum("secd,edf->secf", blocks, w_gate, preferred_element_type=jnp.float32)
    up_part = jnp.einsum("secd,edf->secf", blocks, w_up, preferred_element_type=jnp.float32)
    inner = (jax.nn.silu(gate_part) * up_part).astype(jnp.bfloat16)
    return jnp.einsum("secf,efd->secd", inner, w_down, preferred_element_type=jnp.float32).astype(
        jnp.bfloat16
    )


def routed(normed, expert_ids, gate_weights, w_gate, w_up, w_down, capacity):
    devices = lax.axis_size("ep")
    local_count = w_gate.shape[0]
    experts = devices * local_count
    width = normed.shape[1]
    row_count, top_count = expert_ids.shape
    flat_ids = expert_ids.reshape(-1)
    onehot_table = (flat_ids[:, None] == jnp.arange(experts, dtype=jnp.int32)[None, :]).astype(
        jnp.int32
    )
    before = jnp.cumsum(onehot_table, axis=0) - onehot_table
    slot_index = jnp.sum(before * onehot_table, axis=1)
    target = flat_ids * capacity + slot_index
    target_rows = target.reshape(row_count, top_count)
    placing = jnp.sum(
        (
            target_rows[:, :, None]
            == jnp.arange(experts * capacity, dtype=jnp.int32)[None, None, :]
        ).astype(jnp.float32),
        axis=1,
    ).astype(jnp.bfloat16)
    buffer = jnp.einsum("tp,td->pd", placing, normed, preferred_element_type=jnp.float32).astype(
        jnp.bfloat16
    )
    buffer = buffer.reshape(experts, capacity, width)
    arrived = lax.all_to_all(buffer, "ep", split_axis=0, concat_axis=0, tiled=True)
    item_count = arrived.shape[1]
    blocks = arrived.reshape(devices, local_count, item_count, width)
    finished = expert_work(blocks, w_gate, w_up, w_down).reshape(experts, item_count, width)
    results = lax.all_to_all(finished, "ep", split_axis=0, concat_axis=0, tiled=True)
    picked = jnp.take(results.reshape(experts * capacity, width), target, axis=0)
    picked = picked.reshape(row_count, top_count, width).astype(jnp.float32)
    return jnp.sum(picked * gate_weights[:, :, None], axis=1)


def grid_of(devices):
    cores = 2 if devices % 2 == 0 else 1
    chips = devices // cores
    minor = max(d for d in range(1, chips + 1) if chips % d == 0 and d * d <= chips)
    return chips // minor, minor, cores


def shifted(devices, dz, dy, dc):
    zs, ys, cs = grid_of(devices)
    pairs = []
    for i in range(devices):
        z, y, c = i // (ys * cs), i // cs % ys, i % cs
        to = (((z + dz) % zs) * ys + (y + dy) % ys) * cs + (c + dc) % cs
        pairs.append((i, to))
    return pairs


def send(x, dz, dy, dc):
    return lax.ppermute(x, "ep", shifted(lax.axis_size("ep"), dz, dy, dc))


def gathered(x):
    zs, ys, cs = grid_of(lax.axis_size("ep"))
    pieces = {(0, 0, 0): x}
    for dy in range(1, ys):
        pieces[0, dy, 0] = send(x, 0, dy, 0)
    for dz in sorted(range(1, zs), key=lambda d: -min(d, zs - d)):
        pieces[dz, 0, 0] = send(x, dz, 0, 0)
    for dz in sorted(range(1, zs), key=lambda d: -min(d, zs - d)):
        for dy in range(1, ys):
            pieces[dz, dy, 0] = send(pieces[dz, 0, 0], 0, dy, 0)
    for dz, dy, _ in list(pieces):
        for dc in range(1, cs):
            pieces[dz, dy, dc] = send(pieces[dz, dy, 0], 0, 0, dc)
    return pieces


def reduced(pieces):
    zs, ys, cs = grid_of(lax.axis_size("ep"))

    def joined(own, others):
        total = own.astype(jnp.float32)
        for other in others:
            total = total + other.astype(jnp.float32)
        return total

    order = sorted(range(zs), key=lambda d: -min(d, zs - d))
    by_z = []
    for dz in order:
        by_y = []
        for dy in range(ys):
            arrived = [send(pieces[dz, dy, dc], 0, 0, -dc) for dc in range(1, cs)]
            by_y.append(joined(pieces[dz, dy, 0], arrived))
        arrived = [send(by_y[dy].astype(jnp.bfloat16), 0, -dy, 0) for dy in range(1, ys)]
        by_z.append(joined(by_y[0], arrived))
    arrived = [
        send(part.astype(jnp.bfloat16), -dz, 0, 0) for dz, part in zip(order, by_z) if dz
    ]
    return joined(by_z[order.index(0)], arrived)


LANES = 128


def spread(expert_ids, gate_weights, experts):
    chosen = expert_ids[:, :, None] == jnp.arange(experts, dtype=jnp.int32)[None, None, :]
    table = jnp.sum(jnp.where(chosen, gate_weights[:, :, None], 0.0), axis=1)
    high = lax.reduce_precision(table, 8, 7)
    middle = lax.reduce_precision(table - high, 8, 7)
    low = table - high - middle
    parts = jnp.concatenate([high, middle, low], axis=1).astype(jnp.bfloat16)
    return jnp.pad(parts, ((0, 0), (0, -parts.shape[1] % LANES)))


def dense(normed, expert_ids, gate_weights, w_gate, w_up, w_down):
    devices = lax.axis_size("ep")
    local_count, width = w_gate.shape[:2]
    experts = devices * local_count
    table = spread(expert_ids, gate_weights, experts)
    pieces = gathered(jnp.concatenate([normed, table], axis=1))
    names = list(pieces)
    rows = jnp.concatenate([pieces[name] for name in names], axis=0)
    blocks, table = rows[:, :width], rows[:, width:].astype(jnp.float32)
    total = 0.0
    for local in range(local_count):
        expert = lax.axis_index("ep") * local_count + local
        column = jnp.arange(table.shape[1], dtype=jnp.int32)
        mine = (column % experts == expert) & (column < 3 * experts)
        weight = jnp.sum(jnp.where(mine[None, :], table, 0.0), axis=1)
        gate_part = jnp.dot(blocks, w_gate[local], preferred_element_type=jnp.float32)
        up_part = jnp.dot(blocks, w_up[local], preferred_element_type=jnp.float32)
        inner = (jax.nn.silu(gate_part) * up_part).astype(jnp.bfloat16)
        out = jnp.dot(inner, w_down[local], preferred_element_type=jnp.float32)
        total = total + weight[:, None] * out.astype(jnp.bfloat16).astype(jnp.float32)
    total = total.astype(jnp.bfloat16).reshape(len(names), -1, width)
    return reduced({name: total[i] for i, name in enumerate(names)})


def layer_rows(
    hidden_in,
    queries,
    stored_keys,
    stored_values,
    stored_lengths,
    norm_gain,
    expert_ids,
    gate_weights,
    w_gate,
    w_up,
    w_down,
    capacity,
):
    attention_output = cached_attention(
        queries, stored_keys, stored_values, stored_lengths, QUERY_HEADS, KEY_VALUE_HEADS
    )
    resid = hidden_in.astype(jnp.float32) + attention_output
    mean_square = jnp.mean(resid * resid, axis=-1, keepdims=True)
    normed = (resid * lax.rsqrt(mean_square + 1e-06) * norm_gain[None, :]).astype(jnp.bfloat16)
    experts = lax.axis_size("ep") * w_gate.shape[0]
    if 2 * expert_ids.shape[1] >= experts:
        mixture = dense(normed, expert_ids, gate_weights, w_gate, w_up, w_down)
    else:
        mixture = routed(normed, expert_ids, gate_weights, w_gate, w_up, w_down, capacity)
    return (resid + mixture).astype(jnp.bfloat16)


def local(
    hidden_in,
    queries,
    stored_keys,
    stored_values,
    stored_lengths,
    norm_gain,
    expert_ids,
    gate_weights,
    w_gate,
    w_up,
    w_down,
):
    experts = lax.axis_size("ep") * w_gate.shape[0]
    top_count = expert_ids.shape[1]
    capacity = max(2, 3 * MB_ROWS * top_count // (2 * experts))
    return layer_rows(
        hidden_in,
        queries,
        stored_keys,
        stored_values,
        stored_lengths,
        norm_gain,
        expert_ids,
        gate_weights,
        w_gate,
        w_up,
        w_down,
        MB * capacity,
    )


def solution(mesh):
    in_specs = (
        P(("groups", "ep"), None),
        P(("groups", "ep"), None),
        P(("groups", "ep"), None, None),
        P(("groups", "ep"), None, None),
        P(("groups", "ep")),
        P(),
        P(("groups", "ep"), None),
        P(("groups", "ep"), None),
        P("ep", None, None),
        P("ep", None, None),
        P("ep", None, None),
    )
    out_specs = P(("groups", "ep"), None)
    return jax.shard_map(local, mesh=mesh, in_specs=in_specs, out_specs=out_specs, check_vma=False)
```

```python
import functools
import math

import jax
import jax.numpy as jnp
from jax import lax
from jax.experimental import pallas as pl
from jax.experimental.pallas import tpu as pltpu
from jax.sharding import PartitionSpec as P

QUERY_HEADS = 16
KEY_VALUE_HEADS = 2
MB = 2
MB_ROWS = 16


def cached_attention(queries, stored_keys, stored_values, stored_lengths, heads, kv_heads):
    row_count = queries.shape[0]
    slots = stored_keys.shape[1]
    head_size = queries.shape[1] // heads
    query_head_rows = queries.reshape(row_count, kv_heads, heads // kv_heads, head_size)
    key_head_rows = stored_keys.reshape(row_count, slots, kv_heads, head_size)
    value_head_rows = stored_values.reshape(row_count, slots, kv_heads, head_size)
    scores = jnp.einsum(
        "nkgd,nckd->nkgc", query_head_rows, key_head_rows, preferred_element_type=jnp.float32
    ) / math.sqrt(head_size)
    visible = jnp.arange(slots, dtype=jnp.int32)[None, :] < stored_lengths[:, None]
    visible = visible[:, None, None, :]
    scores = jnp.where(visible, scores, -1e30)
    top_score = jnp.max(scores, axis=-1, keepdims=True)
    expo = jnp.where(visible, jnp.exp(scores - top_score), 0.0)
    probs = (expo / jnp.sum(expo, axis=-1, keepdims=True)).astype(jnp.bfloat16)
    attention_output = jnp.einsum(
        "nkgc,nckd->nkgd", probs, value_head_rows, preferred_element_type=jnp.float32
    )
    return attention_output.reshape(row_count, heads * head_size)


def expert_work(blocks, w_gate, w_up, w_down):
    gate_part = jnp.einsum("secd,edf->secf", blocks, w_gate, preferred_element_type=jnp.float32)
    up_part = jnp.einsum("secd,edf->secf", blocks, w_up, preferred_element_type=jnp.float32)
    inner = (jax.nn.silu(gate_part) * up_part).astype(jnp.bfloat16)
    return jnp.einsum("secf,efd->secd", inner, w_down, preferred_element_type=jnp.float32).astype(
        jnp.bfloat16
    )


def routed(normed, expert_ids, gate_weights, w_gate, w_up, w_down, capacity):
    devices = lax.axis_size("ep")
    local_count = w_gate.shape[0]
    experts = devices * local_count
    width = normed.shape[1]
    row_count, top_count = expert_ids.shape
    flat_ids = expert_ids.reshape(-1)
    onehot_table = (flat_ids[:, None] == jnp.arange(experts, dtype=jnp.int32)[None, :]).astype(
        jnp.int32
    )
    before = jnp.cumsum(onehot_table, axis=0) - onehot_table
    slot_index = jnp.sum(before * onehot_table, axis=1)
    target = flat_ids * capacity + slot_index
    target_rows = target.reshape(row_count, top_count)
    placing = jnp.sum(
        (
            target_rows[:, :, None]
            == jnp.arange(experts * capacity, dtype=jnp.int32)[None, None, :]
        ).astype(jnp.float32),
        axis=1,
    ).astype(jnp.bfloat16)
    buffer = jnp.einsum("tp,td->pd", placing, normed, preferred_element_type=jnp.float32).astype(
        jnp.bfloat16
    )
    buffer = buffer.reshape(experts, capacity, width)
    arrived = lax.all_to_all(buffer, "ep", split_axis=0, concat_axis=0, tiled=True)
    item_count = arrived.shape[1]
    blocks = arrived.reshape(devices, local_count, item_count, width)
    finished = expert_work(blocks, w_gate, w_up, w_down).reshape(experts, item_count, width)
    results = lax.all_to_all(finished, "ep", split_axis=0, concat_axis=0, tiled=True)
    picked = jnp.take(results.reshape(experts * capacity, width), target, axis=0)
    picked = picked.reshape(row_count, top_count, width).astype(jnp.float32)
    return jnp.sum(picked * gate_weights[:, :, None], axis=1)


def grid_of(devices):
    cores = 2 if devices % 2 == 0 else 1
    chips = devices // cores
    minor = max(d for d in range(1, chips + 1) if chips % d == 0 and d * d <= chips)
    return chips // minor, minor, cores


def shifted(devices, dz, dy, dc):
    zs, ys, cs = grid_of(devices)
    pairs = []
    for i in range(devices):
        z, y, c = i // (ys * cs), i // cs % ys, i % cs
        to = (((z + dz) % zs) * ys + (y + dy) % ys) * cs + (c + dc) % cs
        pairs.append((i, to))
    return pairs


def send(x, dz, dy, dc):
    return lax.ppermute(x, "ep", shifted(lax.axis_size("ep"), dz, dy, dc))


def far_first(zs):
    return sorted(range(zs), key=lambda d: (-min(d, zs - d), d))


def gathered(x):
    zs, ys, cs = grid_of(lax.axis_size("ep"))
    pieces = {(0, 0, 0): x}
    for dy in range(1, ys):
        pieces[0, dy, 0] = send(x, 0, dy, 0)
    for dz in far_first(zs):
        if dz:
            pieces[dz, 0, 0] = send(x, dz, 0, 0)
    for dz in far_first(zs):
        for dy in range(1, ys):
            if dz:
                pieces[dz, dy, 0] = send(pieces[dz, 0, 0], 0, dy, 0)
    for dz, dy, _ in list(pieces):
        for dc in range(1, cs):
            pieces[dz, dy, dc] = send(pieces[dz, dy, 0], 0, 0, dc)
    return pieces


LANES = 128
MIB = 1 << 20


def attention_body(
    lengths, hidden, queries, keys, values, gain, ids, gates, payload, resid, parts, *, experts
):
    rows, width = hidden.shape
    _, slots, kv_width = keys.shape
    head = LANES
    kv_heads = kv_width // head
    heads = width // head
    group = heads // kv_heads
    step = pl.program_id(0)
    pair = LANES // slots
    scale = 1.0 / math.sqrt(head)
    f32 = jnp.float32

    blocks = []
    for g in range(kv_heads):
        own = jnp.concatenate(
            [queries[:, h * head : (h + 1) * head] for h in range(g * group, (g + 1) * group)],
            axis=0,
        )
        blank = jnp.zeros_like(own)
        blocks.append(
            jnp.concatenate([own if i == g else blank for i in range(kv_heads)], axis=1)
        )
    stacked = jnp.concatenate(blocks, axis=0)
    flat_keys = keys[...].reshape(rows * slots, kv_width)
    flat_values = values[...].reshape(rows * slots, kv_width)
    scores = lax.dot_general(
        stacked, flat_keys, (((1,), (1,)), ((), ())), preferred_element_type=f32
    )

    request = lax.broadcasted_iota(jnp.int32, (rows, LANES), 0)
    lane = lax.broadcasted_iota(jnp.int32, (rows, LANES), 1)
    length = jnp.zeros((rows, LANES), jnp.int32)
    for t in range(rows):
        length = jnp.where(request == t, lengths[step * rows + t], length)
    seen = (lane // slots == request % pair) & (lane % slots < length)
    seen = jnp.concatenate([seen.astype(jnp.int32)] * heads, axis=0) != 0
    slab = jnp.concatenate([request // pair] * heads, axis=0)
    compact = scores[:, :LANES]
    for j in range(1, rows // pair):
        compact = jnp.where(slab == j, scores[:, j * LANES : (j + 1) * LANES], compact)
    compact = jnp.where(seen, compact * scale, -1e30)
    top = jnp.max(compact, axis=-1, keepdims=True)
    expo = jnp.where(seen, jnp.exp(compact - top), 0.0)
    probs = (expo / jnp.sum(expo, axis=-1, keepdims=True)).astype(jnp.bfloat16)
    probs = probs.astype(f32)
    wide = jnp.concatenate(
        [jnp.where(slab == j, probs, 0.0).astype(jnp.bfloat16) for j in range(rows // pair)],
        axis=1,
    )
    attended = jnp.dot(wide, flat_values, preferred_element_type=f32)

    square = jnp.zeros((rows, LANES), f32)
    for h in range(heads):
        g = h // group
        cols = slice(h * head, (h + 1) * head)
        total = hidden[:, cols].astype(f32)
        total = total + attended[h * rows : (h + 1) * rows, g * head : (g + 1) * head]
        resid[:, cols] = total
        square = square + total * total
    mean_square = jnp.sum(square, axis=-1, keepdims=True) / width
    inverse = lax.rsqrt(mean_square + 1e-06)
    for h in range(heads):
        cols = slice(h * head, (h + 1) * head)
        payload[:, cols] = (resid[:, cols] * inverse * gain[:, cols]).astype(jnp.bfloat16)

    all_rows = ids.shape[1]
    top_count = ids.shape[0]
    number = lax.broadcasted_iota(jnp.int32, (experts, all_rows), 0)
    table = jnp.zeros((experts, all_rows), f32)
    for k in range(top_count):
        table = table + jnp.where(ids[k : k + 1, :] == number, gates[k : k + 1, :], 0.0)
    high = table.astype(jnp.bfloat16).astype(f32)
    middle = (table - high).astype(jnp.bfloat16).astype(f32)
    low = table - high - middle
    parts[...] = jnp.zeros_like(parts)
    for i, part in enumerate((high, middle, low)):
        parts[i * experts : (i + 1) * experts, :all_rows] = part
    flipped = parts[...].T.astype(jnp.bfloat16)

    for i in range(all_rows // rows):

        @pl.when(step == i)
        def _():
            payload[:, width:] = flipped[i * rows : (i + 1) * rows, :]


def attention(
    hidden_in, queries, stored_keys, stored_values, stored_lengths, norm_gain, expert_ids,
    gate_weights, experts,
):
    rows, width = hidden_in.shape
    _, slots, kv_width = stored_keys.shape
    block = MB_ROWS
    whole = width + LANES

    def row(columns):
        return pl.BlockSpec((block, columns), lambda i, n: (i, 0))

    def cache():
        return pl.BlockSpec((block, slots, kv_width), lambda i, n: (i, 0, 0))

    def full(shape):
        return pl.BlockSpec(shape, lambda i, n: (0, 0))

    return pl.pallas_call(
        functools.partial(attention_body, experts=experts),
        out_shape=(
            jax.ShapeDtypeStruct((rows, whole), jnp.bfloat16),
            jax.ShapeDtypeStruct((rows, width), jnp.float32),
        ),
        grid_spec=pltpu.PrefetchScalarGridSpec(
            num_scalar_prefetch=1,
            grid=(rows // block,),
            in_specs=[
                row(width),
                row(width),
                cache(),
                cache(),
                full((1, width)),
                full((expert_ids.shape[1], rows)),
                full((expert_ids.shape[1], rows)),
            ],
            out_specs=(row(whole), row(width)),
            scratch_shapes=[pltpu.VMEM((LANES, LANES), jnp.float32)],
        ),
        compiler_params=pltpu.CompilerParams(vmem_limit_bytes=16 * MIB),
        name="attention",
    )(
        stored_lengths,
        hidden_in,
        queries,
        stored_keys,
        stored_values,
        norm_gain[None, :],
        expert_ids.T,
        gate_weights.T,
    )


TILE = 256


def expert_body(*refs, count, experts, local_count):
    pieces = refs[:count]
    w_gate, w_up, w_down, away, kept, inner, weight = refs[count:]
    width = w_gate.shape[1]
    hidden = w_gate.shape[2]
    rows = pieces[0].shape[0]
    f32 = jnp.float32
    x = jnp.concatenate([piece[:, :width] for piece in pieces], axis=0)
    table = jnp.concatenate([piece[:, width:] for piece in pieces], axis=0).astype(f32)
    lane = lax.broadcasted_iota(jnp.int32, table.shape, 1)
    for local in range(local_count):
        expert = lax.axis_index("ep") * local_count + local
        mine = (
            (lane == expert) | (lane == expert + experts) | (lane == expert + 2 * experts)
        )
        weight[...] = jnp.broadcast_to(
            jnp.sum(jnp.where(mine, table, 0.0), axis=1, keepdims=True), weight.shape
        )
        for f in range(0, hidden, TILE):
            cols = slice(f, f + TILE)
            gate_part = jnp.dot(x, w_gate[local, :, cols], preferred_element_type=f32)
            up_part = jnp.dot(x, w_up[local, :, cols], preferred_element_type=f32)
            silu = gate_part / (1.0 + jnp.exp(-gate_part))
            inner[:, cols] = (silu * up_part).astype(jnp.bfloat16)
        mid = inner[...]
        half = count // 2 * rows
        for d in range(0, width, TILE):
            cols = slice(d, d + TILE)
            out = jnp.dot(mid, w_down[local, :, cols], preferred_element_type=f32)
            out = out.astype(jnp.bfloat16).astype(f32)
            for j in range(0, TILE, LANES):
                part = slice(d + j, d + j + LANES)
                scaled = out[:, j : j + LANES] * weight[...]
                if local == 0:
                    away_sum, kept_sum = scaled[:half], scaled[half:]
                else:
                    away_sum = away[:, part].astype(f32) + scaled[:half]
                    kept_sum = kept[:, part] + scaled[half:]
                away[:, part] = away_sum.astype(away.dtype)
                kept[:, part] = kept_sum


def expert_rows(pieces, w_gate, w_up, w_down, experts):
    rows = pieces[0].shape[0]
    local_count, width, hidden = w_gate.shape
    count = len(pieces)
    half = count // 2 * rows
    vmem = pl.BlockSpec(memory_space=pltpu.VMEM)
    return pl.pallas_call(
        functools.partial(
            expert_body, count=count, experts=experts, local_count=local_count
        ),
        out_shape=(
            jax.ShapeDtypeStruct((half, width), jnp.bfloat16),
            jax.ShapeDtypeStruct((count * rows - half, width), jnp.float32),
        ),
        in_specs=[vmem] * (count + 3),
        out_specs=(vmem, vmem),
        scratch_shapes=[
            pltpu.VMEM((count * rows, hidden), jnp.bfloat16),
            pltpu.VMEM((count * rows, LANES), jnp.float32),
        ],
        compiler_params=pltpu.CompilerParams(vmem_limit_bytes=40 * MIB),
        cost_estimate=pl.CostEstimate(
            flops=6 * count * rows * width * hidden * local_count,
            bytes_accessed=6 * width * hidden * local_count,
            transcendentals=count * rows * hidden,
        ),
        name="expert_rows",
    )(*pieces, w_gate, w_up, w_down)


def dense(payload, resid, w_gate, w_up, w_down):
    devices = lax.axis_size("ep")
    local_count, width = w_gate.shape[:2]
    experts = devices * local_count
    zs, ys, cs = grid_of(devices)
    bf16, f32 = jnp.bfloat16, jnp.float32
    rows = payload.shape[0]
    pieces = gathered(payload)
    order = far_first(zs)
    near = [dz for dz in order if dz in (0, zs // 2)]
    rest = [dz for dz in order if dz not in near]
    total = resid
    for chunk in (near, rest):
        if not chunk:
            continue
        dys = list(range(1, ys)) + [0]
        names = [(dz, dy, dc) for dc in (1, 0) for dy in dys for dz in chunk]
        away, kept = expert_rows(
            [pieces[name] for name in names], w_gate, w_up, w_down, experts
        )
        chip = kept + send(away, 0, 0, 1).astype(f32)
        span = len(chunk) * rows
        level = chip[(ys - 1) * span :]
        for i, dy in enumerate(range(1, ys)):
            level = level + send(
                chip[i * span : (i + 1) * span].astype(bf16), 0, -dy, 0
            ).astype(f32)
        for i, dz in enumerate(chunk):
            part = level[i * rows : (i + 1) * rows]
            total = total + (send(part.astype(bf16), -dz, 0, 0).astype(f32) if dz else part)
    return total.astype(bf16)


def layer_rows(
    hidden_in,
    queries,
    stored_keys,
    stored_values,
    stored_lengths,
    norm_gain,
    expert_ids,
    gate_weights,
    w_gate,
    w_up,
    w_down,
    capacity,
):
    devices = lax.axis_size("ep")
    experts = devices * w_gate.shape[0]
    if 2 * expert_ids.shape[1] >= experts and grid_of(devices)[2] == 2 and 3 * experts <= LANES:
        payload, resid = attention(
            hidden_in, queries, stored_keys, stored_values, stored_lengths, norm_gain,
            expert_ids, gate_weights, experts,
        )
        return dense(payload, resid, w_gate, w_up, w_down)
    attention_output = cached_attention(
        queries, stored_keys, stored_values, stored_lengths, QUERY_HEADS, KEY_VALUE_HEADS
    )
    resid = hidden_in.astype(jnp.float32) + attention_output
    mean_square = jnp.mean(resid * resid, axis=-1, keepdims=True)
    normed = (resid * lax.rsqrt(mean_square + 1e-06) * norm_gain[None, :]).astype(jnp.bfloat16)
    mixture = routed(normed, expert_ids, gate_weights, w_gate, w_up, w_down, capacity)
    return (resid + mixture).astype(jnp.bfloat16)


def local(
    hidden_in,
    queries,
    stored_keys,
    stored_values,
    stored_lengths,
    norm_gain,
    expert_ids,
    gate_weights,
    w_gate,
    w_up,
    w_down,
):
    experts = lax.axis_size("ep") * w_gate.shape[0]
    top_count = expert_ids.shape[1]
    capacity = max(2, 3 * MB_ROWS * top_count // (2 * experts))
    return layer_rows(
        hidden_in,
        queries,
        stored_keys,
        stored_values,
        stored_lengths,
        norm_gain,
        expert_ids,
        gate_weights,
        w_gate,
        w_up,
        w_down,
        MB * capacity,
    )


def solution(mesh):
    in_specs = (
        P(("groups", "ep"), None),
        P(("groups", "ep"), None),
        P(("groups", "ep"), None, None),
        P(("groups", "ep"), None, None),
        P(("groups", "ep")),
        P(),
        P(("groups", "ep"), None),
        P(("groups", "ep"), None),
        P("ep", None, None),
        P("ep", None, None),
        P("ep", None, None),
    )
    out_specs = P(("groups", "ep"), None)
    return jax.shard_map(local, mesh=mesh, in_specs=in_specs, out_specs=out_specs, check_vma=False)
```

```python
import functools
import math

import jax
import jax.numpy as jnp
from jax import lax
from jax.experimental import pallas as pl
from jax.experimental.pallas import tpu as pltpu
from jax.sharding import PartitionSpec as P


QUERY_HEADS = 16
KEY_VALUE_HEADS = 2
MB = 2
MB_ROWS = 16


def cached_attention(queries, stored_keys, stored_values, stored_lengths, heads, kv_heads):
    row_count = queries.shape[0]
    slots = stored_keys.shape[1]
    head_size = queries.shape[1] // heads
    query_head_rows = queries.reshape(row_count, kv_heads, heads // kv_heads, head_size)
    key_head_rows = stored_keys.reshape(row_count, slots, kv_heads, head_size)
    value_head_rows = stored_values.reshape(row_count, slots, kv_heads, head_size)
    scores = jnp.einsum(
        "nkgd,nckd->nkgc", query_head_rows, key_head_rows, preferred_element_type=jnp.float32
    ) / math.sqrt(head_size)
    visible = jnp.arange(slots, dtype=jnp.int32)[None, :] < stored_lengths[:, None]
    visible = visible[:, None, None, :]
    scores = jnp.where(visible, scores, -1e30)
    top_score = jnp.max(scores, axis=-1, keepdims=True)
    expo = jnp.where(visible, jnp.exp(scores - top_score), 0.0)
    probs = (expo / jnp.sum(expo, axis=-1, keepdims=True)).astype(jnp.bfloat16)
    attention_output = jnp.einsum(
        "nkgc,nckd->nkgd", probs, value_head_rows, preferred_element_type=jnp.float32
    )
    return attention_output.reshape(row_count, heads * head_size)


def expert_work(blocks, w_gate, w_up, w_down):
    gate_part = jnp.einsum("secd,edf->secf", blocks, w_gate, preferred_element_type=jnp.float32)
    up_part = jnp.einsum("secd,edf->secf", blocks, w_up, preferred_element_type=jnp.float32)
    inner = (jax.nn.silu(gate_part) * up_part).astype(jnp.bfloat16)
    return jnp.einsum("secf,efd->secd", inner, w_down, preferred_element_type=jnp.float32).astype(
        jnp.bfloat16
    )


def routed(normed, expert_ids, gate_weights, w_gate, w_up, w_down, capacity):
    devices = lax.axis_size("ep")
    local_count = w_gate.shape[0]
    experts = devices * local_count
    width = normed.shape[1]
    row_count, top_count = expert_ids.shape
    flat_ids = expert_ids.reshape(-1)
    onehot_table = (flat_ids[:, None] == jnp.arange(experts, dtype=jnp.int32)[None, :]).astype(
        jnp.int32
    )
    before = jnp.cumsum(onehot_table, axis=0) - onehot_table
    slot_index = jnp.sum(before * onehot_table, axis=1)
    target = flat_ids * capacity + slot_index
    target_rows = target.reshape(row_count, top_count)
    placing = jnp.sum(
        (
            target_rows[:, :, None]
            == jnp.arange(experts * capacity, dtype=jnp.int32)[None, None, :]
        ).astype(jnp.float32),
        axis=1,
    ).astype(jnp.bfloat16)
    buffer = jnp.einsum("tp,td->pd", placing, normed, preferred_element_type=jnp.float32).astype(
        jnp.bfloat16
    )
    buffer = buffer.reshape(experts, capacity, width)
    arrived = lax.all_to_all(buffer, "ep", split_axis=0, concat_axis=0, tiled=True)
    item_count = arrived.shape[1]
    blocks = arrived.reshape(devices, local_count, item_count, width)
    finished = expert_work(blocks, w_gate, w_up, w_down).reshape(experts, item_count, width)
    results = lax.all_to_all(finished, "ep", split_axis=0, concat_axis=0, tiled=True)
    picked = jnp.take(results.reshape(experts * capacity, width), target, axis=0)
    picked = picked.reshape(row_count, top_count, width).astype(jnp.float32)
    return jnp.sum(picked * gate_weights[:, :, None], axis=1)


def grid_of(devices):
    cores = 2 if devices % 2 == 0 else 1
    chips = devices // cores
    minor = max(d for d in range(1, chips + 1) if chips % d == 0 and d * d <= chips)
    return chips // minor, minor, cores


def shifted(devices, dz, dy, dc):
    zs, ys, cs = grid_of(devices)
    pairs = []
    for i in range(devices):
        z, y, c = i // (ys * cs), i // cs % ys, i % cs
        to = (((z + dz) % zs) * ys + (y + dy) % ys) * cs + (c + dc) % cs
        pairs.append((i, to))
    return pairs


def send(x, dz, dy, dc):
    return lax.ppermute(x, "ep", shifted(lax.axis_size("ep"), dz, dy, dc))


def far_first(zs):
    return sorted(range(zs), key=lambda d: (-min(d, zs - d), d))


def gathered(x):
    zs, ys, cs = grid_of(lax.axis_size("ep"))
    pieces = {(0, 0, 0): x}
    for dz in far_first(zs):
        if dz:
            pieces[dz, 0, 0] = send(x, dz, 0, 0)
    for dz in range(zs):
        for dy in range(1, ys):
            pieces[dz, dy, 0] = send(pieces[dz, 0, 0], 0, dy, 0)
    for dz, dy, _ in list(pieces):
        for dc in range(1, cs):
            pieces[dz, dy, dc] = send(pieces[dz, dy, 0], 0, 0, dc)
    return pieces


LANES = 128
MIB = 1 << 20


def attention_body(
    lengths_in, hidden_in, queries_in, keys_in, values_in, gain_in, ids_in, gates_in,
    payload, resid,
    lengths, hidden, queries, keys, values, gain, ids, gates, parts, sems, *, experts,
):
    rows, width = hidden.shape
    _, slots, kv_width = keys.shape
    head = LANES
    kv_heads = kv_width // head
    heads = width // head
    group = heads // kv_heads
    block = MB_ROWS
    pair = LANES // slots
    scale = 1.0 / math.sqrt(head)
    f32 = jnp.float32

    copies = {}

    def fetch(name, source, target):
        copies[name] = pltpu.make_async_copy(source, target, sems.at[len(copies)])
        copies[name].start()

    fetch("queries", queries_in, queries)
    for b in range(rows // block):
        at = pl.ds(b * block, block)
        fetch(("keys", b), keys_in.at[at], keys.at[at])
        if b == 0:
            fetch("lengths", lengths_in, lengths)
            fetch("ids", ids_in, ids)
            fetch("gates", gates_in, gates)
        fetch(("values", b), values_in.at[at], values.at[at])
        if b == 0:
            fetch("hidden", hidden_in, hidden)
            fetch("gain", gain_in, gain)

    copies["ids"].wait()
    copies["gates"].wait()
    number = lax.broadcasted_iota(jnp.int32, (experts, rows), 0)
    table = jnp.zeros((experts, rows), f32)
    for k in range(ids.shape[0]):
        table = table + jnp.where(ids[k : k + 1, :] == number, gates[k : k + 1, :], 0.0)
    high = table.astype(jnp.bfloat16).astype(f32)
    middle = (table - high).astype(jnp.bfloat16).astype(f32)
    low = table - high - middle
    parts[...] = jnp.zeros_like(parts)
    for i, part in enumerate((high, middle, low)):
        parts[i * experts : (i + 1) * experts, :rows] = part
    payload[:, width:] = parts[...].T[:rows].astype(jnp.bfloat16)

    copies["lengths"].wait()
    copies["queries"].wait()
    request = lax.broadcasted_iota(jnp.int32, (block, LANES), 0)
    lane = lax.broadcasted_iota(jnp.int32, (block, LANES), 1)
    slab = jnp.concatenate([request // pair] * heads, axis=0)
    for b in range(rows // block):
        at = slice(b * block, (b + 1) * block)
        blocks = []
        for g in range(kv_heads):
            own = jnp.concatenate(
                [
                    queries[at, h * head : (h + 1) * head]
                    for h in range(g * group, (g + 1) * group)
                ],
                axis=0,
            )
            blank = jnp.zeros_like(own)
            blocks.append(
                jnp.concatenate([own if i == g else blank for i in range(kv_heads)], axis=1)
            )
        stacked = jnp.concatenate(blocks, axis=0)
        copies["keys", b].wait()
        scores = lax.dot_general(
            stacked,
            keys[at].reshape(block * slots, kv_width),
            (((1,), (1,)), ((), ())),
            preferred_element_type=f32,
        )

        length = jnp.zeros((block, LANES), jnp.int32)
        for t in range(block):
            length = jnp.where(request == t, lengths[b * block + t], length)
        seen = (lane // slots == request % pair) & (lane % slots < length)
        seen = jnp.concatenate([seen.astype(jnp.int32)] * heads, axis=0) != 0
        compact = scores[:, :LANES]
        for j in range(1, block // pair):
            compact = jnp.where(slab == j, scores[:, j * LANES : (j + 1) * LANES], compact)
        compact = jnp.where(seen, compact * scale, -1e30)
        top = jnp.max(compact, axis=-1, keepdims=True)
        expo = jnp.where(seen, jnp.exp(compact - top), 0.0)
        probs = (expo / jnp.sum(expo, axis=-1, keepdims=True)).astype(jnp.bfloat16)
        probs = probs.astype(f32)
        wide = jnp.concatenate(
            [jnp.where(slab == j, probs, 0.0).astype(jnp.bfloat16) for j in range(block // pair)],
            axis=1,
        )
        copies["values", b].wait()
        attended = jnp.dot(
            wide, values[at].reshape(block * slots, kv_width), preferred_element_type=f32
        )

        if b == 0:
            copies["hidden"].wait()
            copies["gain"].wait()
        square = jnp.zeros((block, LANES), f32)
        for h in range(heads):
            g = h // group
            cols = slice(h * head, (h + 1) * head)
            total = hidden[at, cols].astype(f32)
            total = total + attended[h * block : (h + 1) * block, g * head : (g + 1) * head]
            resid[at, cols] = total
            square = square + total * total
        mean_square = jnp.sum(square, axis=-1, keepdims=True) / width
        inverse = lax.rsqrt(mean_square + 1e-06)
        for h in range(heads):
            cols = slice(h * head, (h + 1) * head)
            payload[at, cols] = (resid[at, cols] * inverse * gain[:, cols]).astype(jnp.bfloat16)


def attention(
    hidden_in, queries, stored_keys, stored_values, stored_lengths, norm_gain, expert_ids,
    gate_weights, experts,
):
    rows, width = hidden_in.shape
    whole = width + LANES
    vmem = pl.BlockSpec(memory_space=pltpu.VMEM)
    operands = (
        stored_lengths,
        hidden_in,
        queries,
        stored_keys,
        stored_values,
        norm_gain[None, :],
        expert_ids.T,
        gate_weights.T,
    )
    return pl.pallas_call(
        functools.partial(attention_body, experts=experts),
        out_shape=(
            jax.ShapeDtypeStruct((rows, whole), jnp.bfloat16),
            jax.ShapeDtypeStruct((rows, width), jnp.float32),
        ),
        in_specs=[pl.BlockSpec(memory_space=pltpu.HBM)] * len(operands),
        out_specs=(vmem, vmem),
        scratch_shapes=[
            pltpu.SMEM(operands[0].shape, operands[0].dtype),
            *(pltpu.VMEM(x.shape, x.dtype) for x in operands[1:]),
            pltpu.VMEM((LANES, LANES), jnp.float32),
            pltpu.SemaphoreType.DMA((6 + 2 * (rows // MB_ROWS),)),
        ],
        compiler_params=pltpu.CompilerParams(vmem_limit_bytes=16 * MIB),
        name="attention",
    )(*(pltpu.with_memory_space_constraint(x, pltpu.HBM) for x in operands))


def loader_body(*refs, count):
    after, sources, targets, sems = refs[0], refs[1 : count + 1], refs[count + 1 : -1], refs[-1]
    del after
    copies = [
        pltpu.make_async_copy(source, target, sems.at[i])
        for i, (source, target) in enumerate(zip(sources, targets))
    ]
    for copy in copies:
        copy.start()
    for copy in copies:
        copy.wait()


def loaded(after, *arrays):
    hbm = pl.BlockSpec(memory_space=pltpu.HBM)
    vmem = pl.BlockSpec(memory_space=pltpu.VMEM)
    return pl.pallas_call(
        functools.partial(loader_body, count=len(arrays)),
        out_shape=tuple(jax.ShapeDtypeStruct(x.shape, x.dtype) for x in arrays),
        in_specs=[pl.BlockSpec(memory_space=pltpu.VMEM)] + [hbm] * len(arrays),
        out_specs=(vmem,) * len(arrays),
        scratch_shapes=[pltpu.SemaphoreType.DMA((len(arrays),))],
        compiler_params=pltpu.CompilerParams(vmem_limit_bytes=16 * MIB),
        cost_estimate=pl.CostEstimate(
            flops=0, bytes_accessed=sum(2 * x.size for x in arrays), transcendentals=0
        ),
        name="loader",
    )(after, *(pltpu.with_memory_space_constraint(x, pltpu.HBM) for x in arrays))


TILE = 256


def expert_body(*refs, count, experts, local_count):
    pieces = refs[:count]
    w_gate, w_up, w_down, away, kept, inner, weight = refs[count:]
    width = w_gate.shape[1]
    hidden = w_gate.shape[2]
    rows = pieces[0].shape[0]
    f32 = jnp.float32
    x = jnp.concatenate([piece[:, :width] for piece in pieces], axis=0)
    table = jnp.concatenate([piece[:, width:] for piece in pieces], axis=0).astype(f32)
    lane = lax.broadcasted_iota(jnp.int32, table.shape, 1)
    for local in range(local_count):
        expert = lax.axis_index("ep") * local_count + local
        mine = (
            (lane == expert) | (lane == expert + experts) | (lane == expert + 2 * experts)
        )
        weight[...] = jnp.broadcast_to(
            jnp.sum(jnp.where(mine, table, 0.0), axis=1, keepdims=True), weight.shape
        )
        for f in range(0, hidden, TILE):
            cols = slice(f, f + TILE)
            gate_part = jnp.dot(x, w_gate[local, :, cols], preferred_element_type=f32)
            up_part = jnp.dot(x, w_up[local, :, cols], preferred_element_type=f32)
            silu = gate_part / (1.0 + jnp.exp(-gate_part))
            inner[:, cols] = (silu * up_part).astype(jnp.bfloat16)
        mid = inner[...]
        half = count // 2 * rows
        for d in range(0, width, TILE):
            cols = slice(d, d + TILE)
            out = jnp.dot(mid, w_down[local, :, cols], preferred_element_type=f32)
            out = out.astype(jnp.bfloat16).astype(f32)
            for j in range(0, TILE, LANES):
                part = slice(d + j, d + j + LANES)
                scaled = out[:, j : j + LANES] * weight[...]
                if local == 0:
                    away_sum, kept_sum = scaled[:half], scaled[half:]
                else:
                    away_sum = away[:, part].astype(f32) + scaled[:half]
                    kept_sum = kept[:, part] + scaled[half:]
                away[:, part] = away_sum.astype(away.dtype)
                kept[:, part] = kept_sum


def expert_rows(pieces, w_gate, w_up, w_down, experts):
    rows = pieces[0].shape[0]
    local_count, width, hidden = w_gate.shape
    count = len(pieces)
    half = count // 2 * rows
    vmem = pl.BlockSpec(memory_space=pltpu.VMEM)
    return pl.pallas_call(
        functools.partial(
            expert_body, count=count, experts=experts, local_count=local_count
        ),
        out_shape=(
            jax.ShapeDtypeStruct((half, width), jnp.bfloat16),
            jax.ShapeDtypeStruct((count * rows - half, width), jnp.float32),
        ),
        in_specs=[vmem] * (count + 3),
        out_specs=(vmem, vmem),
        scratch_shapes=[
            pltpu.VMEM((count * rows, hidden), jnp.bfloat16),
            pltpu.VMEM((count * rows, LANES), jnp.float32),
        ],
        compiler_params=pltpu.CompilerParams(vmem_limit_bytes=16 * MIB),
        cost_estimate=pl.CostEstimate(
            flops=6 * count * rows * width * hidden * local_count,
            bytes_accessed=6 * width * hidden * local_count,
            transcendentals=count * rows * hidden,
        ),
        name="expert_rows",
    )(*pieces, w_gate, w_up, w_down)


def chunks_of(zs):
    order = far_first(zs)
    near = [dz for dz in order if dz in (0, zs // 2)]
    return [chunk for chunk in (near, [dz for dz in order if dz not in near]) if chunk]


def dense(payload, resid, w_gate, w_up, w_down):
    devices = lax.axis_size("ep")
    local_count = w_gate.shape[0]
    experts = devices * local_count
    zs, ys, _ = grid_of(devices)
    bf16, f32 = jnp.bfloat16, jnp.float32
    rows = payload.shape[0]
    pieces = gathered(payload)
    weights = loaded(payload, w_gate, w_up, w_down)
    total = resid
    for chunk in chunks_of(zs):
        dys = list(range(1, ys)) + [0]
        names = [(dz, dy, dc) for dc in (1, 0) for dz in chunk for dy in dys]
        away, kept = expert_rows([pieces[name] for name in names], *weights, experts)
        chip = kept + send(away, 0, 0, 1).astype(f32)
        for i, dz in enumerate(chunk):
            first = i * ys * rows
            level = chip[first + (ys - 1) * rows : first + ys * rows]
            for j, dy in enumerate(dys[:-1]):
                part = chip[first + j * rows : first + (j + 1) * rows].astype(bf16)
                level = level + send(part, 0, -dy, 0).astype(f32)
            if dz:
                level = send(level.astype(bf16), -dz, 0, 0).astype(f32)
            total = total + level
    return total.astype(bf16)


def layer_rows(
    hidden_in,
    queries,
    stored_keys,
    stored_values,
    stored_lengths,
    norm_gain,
    expert_ids,
    gate_weights,
    w_gate,
    w_up,
    w_down,
    capacity,
):
    devices = lax.axis_size("ep")
    experts = devices * w_gate.shape[0]
    if 2 * expert_ids.shape[1] >= experts and grid_of(devices)[2] == 2 and 3 * experts <= LANES:
        payload, resid = attention(
            hidden_in, queries, stored_keys, stored_values, stored_lengths, norm_gain,
            expert_ids, gate_weights, experts,
        )
        return dense(payload, resid, w_gate, w_up, w_down)
    attention_output = cached_attention(
        queries, stored_keys, stored_values, stored_lengths, QUERY_HEADS, KEY_VALUE_HEADS
    )
    resid = hidden_in.astype(jnp.float32) + attention_output
    mean_square = jnp.mean(resid * resid, axis=-1, keepdims=True)
    normed = (resid * lax.rsqrt(mean_square + 1e-06) * norm_gain[None, :]).astype(jnp.bfloat16)
    mixture = routed(normed, expert_ids, gate_weights, w_gate, w_up, w_down, capacity)
    return (resid + mixture).astype(jnp.bfloat16)


def local(
    hidden_in,
    queries,
    stored_keys,
    stored_values,
    stored_lengths,
    norm_gain,
    expert_ids,
    gate_weights,
    w_gate,
    w_up,
    w_down,
):
    experts = lax.axis_size("ep") * w_gate.shape[0]
    top_count = expert_ids.shape[1]
    capacity = max(2, 3 * MB_ROWS * top_count // (2 * experts))
    return layer_rows(
        hidden_in,
        queries,
        stored_keys,
        stored_values,
        stored_lengths,
        norm_gain,
        expert_ids,
        gate_weights,
        w_gate,
        w_up,
        w_down,
        MB * capacity,
    )


def solution(mesh):
    in_specs = (
        P(("groups", "ep"), None),
        P(("groups", "ep"), None),
        P(("groups", "ep"), None, None),
        P(("groups", "ep"), None, None),
        P(("groups", "ep")),
        P(),
        P(("groups", "ep"), None),
        P(("groups", "ep"), None),
        P("ep", None, None),
        P("ep", None, None),
        P("ep", None, None),
    )
    out_specs = P(("groups", "ep"), None)
    return jax.shard_map(local, mesh=mesh, in_specs=in_specs, out_specs=out_specs, check_vma=False)
```

```python
import functools
import math

import jax
import jax.numpy as jnp
from jax import lax
from jax.experimental import pallas as pl
from jax.experimental.pallas import tpu as pltpu
from jax.sharding import PartitionSpec as P


QUERY_HEADS = 16
KEY_VALUE_HEADS = 2
MB = 2
MB_ROWS = 16


def cached_attention(queries, stored_keys, stored_values, stored_lengths, heads, kv_heads):
    row_count = queries.shape[0]
    slots = stored_keys.shape[1]
    head_size = queries.shape[1] // heads
    query_head_rows = queries.reshape(row_count, kv_heads, heads // kv_heads, head_size)
    key_head_rows = stored_keys.reshape(row_count, slots, kv_heads, head_size)
    value_head_rows = stored_values.reshape(row_count, slots, kv_heads, head_size)
    scores = jnp.einsum(
        "nkgd,nckd->nkgc", query_head_rows, key_head_rows, preferred_element_type=jnp.float32
    ) / math.sqrt(head_size)
    visible = jnp.arange(slots, dtype=jnp.int32)[None, :] < stored_lengths[:, None]
    visible = visible[:, None, None, :]
    scores = jnp.where(visible, scores, -1e30)
    top_score = jnp.max(scores, axis=-1, keepdims=True)
    expo = jnp.where(visible, jnp.exp(scores - top_score), 0.0)
    probs = (expo / jnp.sum(expo, axis=-1, keepdims=True)).astype(jnp.bfloat16)
    attention_output = jnp.einsum(
        "nkgc,nckd->nkgd", probs, value_head_rows, preferred_element_type=jnp.float32
    )
    return attention_output.reshape(row_count, heads * head_size)


def expert_work(blocks, w_gate, w_up, w_down):
    gate_part = jnp.einsum("secd,edf->secf", blocks, w_gate, preferred_element_type=jnp.float32)
    up_part = jnp.einsum("secd,edf->secf", blocks, w_up, preferred_element_type=jnp.float32)
    inner = (jax.nn.silu(gate_part) * up_part).astype(jnp.bfloat16)
    return jnp.einsum("secf,efd->secd", inner, w_down, preferred_element_type=jnp.float32).astype(
        jnp.bfloat16
    )


def routed(normed, expert_ids, gate_weights, w_gate, w_up, w_down, capacity):
    devices = lax.axis_size("ep")
    local_count = w_gate.shape[0]
    experts = devices * local_count
    width = normed.shape[1]
    row_count, top_count = expert_ids.shape
    flat_ids = expert_ids.reshape(-1)
    onehot_table = (flat_ids[:, None] == jnp.arange(experts, dtype=jnp.int32)[None, :]).astype(
        jnp.int32
    )
    before = jnp.cumsum(onehot_table, axis=0) - onehot_table
    slot_index = jnp.sum(before * onehot_table, axis=1)
    target = flat_ids * capacity + slot_index
    target_rows = target.reshape(row_count, top_count)
    placing = jnp.sum(
        (
            target_rows[:, :, None]
            == jnp.arange(experts * capacity, dtype=jnp.int32)[None, None, :]
        ).astype(jnp.float32),
        axis=1,
    ).astype(jnp.bfloat16)
    buffer = jnp.einsum("tp,td->pd", placing, normed, preferred_element_type=jnp.float32).astype(
        jnp.bfloat16
    )
    buffer = buffer.reshape(experts, capacity, width)
    arrived = lax.all_to_all(buffer, "ep", split_axis=0, concat_axis=0, tiled=True)
    item_count = arrived.shape[1]
    blocks = arrived.reshape(devices, local_count, item_count, width)
    finished = expert_work(blocks, w_gate, w_up, w_down).reshape(experts, item_count, width)
    results = lax.all_to_all(finished, "ep", split_axis=0, concat_axis=0, tiled=True)
    picked = jnp.take(results.reshape(experts * capacity, width), target, axis=0)
    picked = picked.reshape(row_count, top_count, width).astype(jnp.float32)
    return jnp.sum(picked * gate_weights[:, :, None], axis=1)


def grid_of(devices):
    cores = 2 if devices % 2 == 0 else 1
    chips = devices // cores
    minor = max(d for d in range(1, chips + 1) if chips % d == 0 and d * d <= chips)
    return chips // minor, minor, cores


def dense_fits(devices):
    zs, _, cs = grid_of(devices)
    return devices & (devices - 1) == 0 and zs > 2 and cs == 2


def send(x, dz, dy, dc):
    devices = lax.axis_size("ep")
    _, ys, cs = grid_of(devices)
    mask = (dz * ys + dy) * cs + dc
    return lax.ppermute(x, "ep", [(i, i ^ mask) for i in range(devices)])


def gathered(x):
    zs, ys, cs = grid_of(lax.axis_size("ep"))
    pieces = {(0, 0, 0): x}
    for dz in range(1, zs):
        pieces[dz, 0, 0] = send(x, dz, 0, 0)
    for dz in range(zs):
        for dy in range(1, ys):
            pieces[dz, dy, 0] = send(pieces[dz, 0, 0], 0, dy, 0)
    for dz, dy, _ in list(pieces):
        for dc in range(1, cs):
            pieces[dz, dy, dc] = send(pieces[dz, dy, 0], 0, 0, dc)
    return pieces


LANES = 128
MIB = 1 << 20


def attention_body(
    lengths_in, hidden_in, queries_in, keys_in, values_in, gain_in, ids_in, gates_in,
    w_gate_in,
    payload, resid, w_gate,
    lengths, hidden, queries, keys, values, gain, ids, gates, parts, sems, *, experts,
):
    rows, width = hidden.shape
    _, slots, kv_width = keys.shape
    head = LANES
    kv_heads = kv_width // head
    heads = width // head
    group = heads // kv_heads
    block = MB_ROWS
    pair = LANES // slots
    scale = 1.0 / math.sqrt(head)
    f32 = jnp.float32

    copies = {}

    def fetch(name, source, target):
        copies[name] = pltpu.make_async_copy(source, target, sems.at[len(copies)])
        copies[name].start()

    fetch("queries", queries_in, queries)
    for b in range(rows // block):
        at = pl.ds(b * block, block)
        fetch(("keys", b), keys_in.at[at], keys.at[at])
        if b == 0:
            fetch("lengths", lengths_in, lengths)
            fetch("ids", ids_in, ids)
            fetch("gates", gates_in, gates)
        fetch(("values", b), values_in.at[at], values.at[at])
        if b == 0:
            fetch("hidden", hidden_in, hidden)
            fetch("gain", gain_in, gain)
    fetch("w_gate", w_gate_in, w_gate)

    copies["ids"].wait()
    copies["gates"].wait()
    number = lax.broadcasted_iota(jnp.int32, (experts, rows), 0)
    table = jnp.zeros((experts, rows), f32)
    for k in range(ids.shape[0]):
        table = table + jnp.where(ids[k : k + 1, :] == number, gates[k : k + 1, :], 0.0)
    high = table.astype(jnp.bfloat16).astype(f32)
    middle = (table - high).astype(jnp.bfloat16).astype(f32)
    low = table - high - middle
    parts[...] = jnp.zeros_like(parts)
    for i, part in enumerate((high, middle, low)):
        parts[i * experts : (i + 1) * experts, :rows] = part
    payload[:, width:] = parts[...].T[:rows].astype(jnp.bfloat16)

    copies["lengths"].wait()
    copies["queries"].wait()
    request = lax.broadcasted_iota(jnp.int32, (block, LANES), 0)
    lane = lax.broadcasted_iota(jnp.int32, (block, LANES), 1)
    slab = jnp.concatenate([request // pair] * heads, axis=0)
    for b in range(rows // block):
        at = slice(b * block, (b + 1) * block)
        blocks = []
        for g in range(kv_heads):
            own = jnp.concatenate(
                [
                    queries[at, h * head : (h + 1) * head]
                    for h in range(g * group, (g + 1) * group)
                ],
                axis=0,
            )
            blank = jnp.zeros_like(own)
            blocks.append(
                jnp.concatenate([own if i == g else blank for i in range(kv_heads)], axis=1)
            )
        stacked = jnp.concatenate(blocks, axis=0)
        copies["keys", b].wait()
        scores = lax.dot_general(
            stacked,
            keys[at].reshape(block * slots, kv_width),
            (((1,), (1,)), ((), ())),
            preferred_element_type=f32,
        )

        length = jnp.zeros((block, LANES), jnp.int32)
        for t in range(block):
            length = jnp.where(request == t, lengths[b * block + t], length)
        seen = (lane // slots == request % pair) & (lane % slots < length)
        seen = jnp.concatenate([seen.astype(jnp.int32)] * heads, axis=0) != 0
        compact = scores[:, :LANES]
        for j in range(1, block // pair):
            compact = jnp.where(slab == j, scores[:, j * LANES : (j + 1) * LANES], compact)
        compact = jnp.where(seen, compact * scale, -1e30)
        top = jnp.max(compact, axis=-1, keepdims=True)
        expo = jnp.where(seen, jnp.exp(compact - top), 0.0)
        probs = (expo / jnp.sum(expo, axis=-1, keepdims=True)).astype(jnp.bfloat16)
        probs = probs.astype(f32)
        wide = jnp.concatenate(
            [jnp.where(slab == j, probs, 0.0).astype(jnp.bfloat16) for j in range(block // pair)],
            axis=1,
        )
        copies["values", b].wait()
        attended = jnp.dot(
            wide, values[at].reshape(block * slots, kv_width), preferred_element_type=f32
        )

        if b == 0:
            copies["hidden"].wait()
            copies["gain"].wait()
        square = jnp.zeros((block, LANES), f32)
        for h in range(heads):
            g = h // group
            cols = slice(h * head, (h + 1) * head)
            total = hidden[at, cols].astype(f32)
            total = total + attended[h * block : (h + 1) * block, g * head : (g + 1) * head]
            resid[at, cols] = total
            square = square + total * total
        mean_square = jnp.sum(square, axis=-1, keepdims=True) / width
        inverse = lax.rsqrt(mean_square + 1e-06)
        for h in range(heads):
            cols = slice(h * head, (h + 1) * head)
            payload[at, cols] = (resid[at, cols] * inverse * gain[:, cols]).astype(jnp.bfloat16)
    copies["w_gate"].wait()


def attention(
    hidden_in, queries, stored_keys, stored_values, stored_lengths, norm_gain, expert_ids,
    gate_weights, w_gate, experts,
):
    rows, width = hidden_in.shape
    whole = width + LANES
    vmem = pl.BlockSpec(memory_space=pltpu.VMEM)
    operands = (
        stored_lengths,
        hidden_in,
        queries,
        stored_keys,
        stored_values,
        norm_gain[None, :],
        expert_ids.T,
        gate_weights.T,
        w_gate,
    )
    return pl.pallas_call(
        functools.partial(attention_body, experts=experts),
        out_shape=(
            jax.ShapeDtypeStruct((rows, whole), jnp.bfloat16),
            jax.ShapeDtypeStruct((rows, width), jnp.float32),
            jax.ShapeDtypeStruct(w_gate.shape, w_gate.dtype),
        ),
        in_specs=[pl.BlockSpec(memory_space=pltpu.HBM)] * len(operands),
        out_specs=(vmem,) * 3,
        scratch_shapes=[
            pltpu.SMEM(operands[0].shape, operands[0].dtype),
            *(pltpu.VMEM(x.shape, x.dtype) for x in operands[1:-1]),
            pltpu.VMEM((LANES, LANES), jnp.float32),
            pltpu.SemaphoreType.DMA((7 + 2 * (rows // MB_ROWS),)),
        ],
        compiler_params=pltpu.CompilerParams(vmem_limit_bytes=16 * MIB),
        name="attention",
    )(*(pltpu.with_memory_space_constraint(x, pltpu.HBM) for x in operands))


def loader_body(after, source, target, sem):
    del after
    copy = pltpu.make_async_copy(source, target, sem)
    copy.start()
    copy.wait()


def loaded(after, x):
    vmem = pl.BlockSpec(memory_space=pltpu.VMEM)
    return pl.pallas_call(
        loader_body,
        out_shape=jax.ShapeDtypeStruct(x.shape, x.dtype),
        in_specs=[vmem, pl.BlockSpec(memory_space=pltpu.HBM)],
        out_specs=vmem,
        scratch_shapes=[pltpu.SemaphoreType.DMA(())],
        compiler_params=pltpu.CompilerParams(vmem_limit_bytes=4 * MIB),
        name="loader",
    )(after, pltpu.with_memory_space_constraint(x, pltpu.HBM))


TILE = 256


def expert_body(*refs, count, experts, local_count):
    pieces = refs[:count]
    w_gate, w_up, w_down, away, kept, inner, weight = refs[count:]
    width = w_gate.shape[1]
    hidden = w_gate.shape[2]
    rows = pieces[0].shape[0]
    f32 = jnp.float32
    x = jnp.concatenate([piece[:, :width] for piece in pieces], axis=0)
    table = jnp.concatenate([piece[:, width:] for piece in pieces], axis=0).astype(f32)
    lane = lax.broadcasted_iota(jnp.int32, table.shape, 1)
    for local in range(local_count):
        expert = lax.axis_index("ep") * local_count + local
        mine = (
            (lane == expert) | (lane == expert + experts) | (lane == expert + 2 * experts)
        )
        weight[...] = jnp.broadcast_to(
            jnp.sum(jnp.where(mine, table, 0.0), axis=1, keepdims=True), weight.shape
        )
        for f in range(0, hidden, TILE):
            cols = slice(f, f + TILE)
            gate_part = jnp.dot(x, w_gate[local, :, cols], preferred_element_type=f32)
            up_part = jnp.dot(x, w_up[local, :, cols], preferred_element_type=f32)
            silu = gate_part / (1.0 + jnp.exp(-gate_part))
            inner[:, cols] = (silu * up_part).astype(jnp.bfloat16)
        mid = inner[...]
        half = count // 2 * rows
        for d in range(0, width, TILE):
            cols = slice(d, d + TILE)
            out = jnp.dot(mid, w_down[local, :, cols], preferred_element_type=f32)
            out = out.astype(jnp.bfloat16).astype(f32)
            for j in range(0, TILE, LANES):
                part = slice(d + j, d + j + LANES)
                scaled = out[:, j : j + LANES] * weight[...]
                if local == 0:
                    away_sum, kept_sum = scaled[:half], scaled[half:]
                else:
                    away_sum = away[:, part].astype(f32) + scaled[:half]
                    kept_sum = kept[:, part] + scaled[half:]
                away[:, part] = away_sum.astype(away.dtype)
                kept[:, part] = kept_sum


def expert_rows(pieces, w_gate, w_up, w_down, experts):
    rows = pieces[0].shape[0]
    local_count, width, hidden = w_gate.shape
    count = len(pieces)
    half = count // 2 * rows
    vmem = pl.BlockSpec(memory_space=pltpu.VMEM)
    return pl.pallas_call(
        functools.partial(
            expert_body, count=count, experts=experts, local_count=local_count
        ),
        out_shape=(
            jax.ShapeDtypeStruct((half, width), jnp.bfloat16),
            jax.ShapeDtypeStruct((count * rows - half, width), jnp.float32),
        ),
        in_specs=[vmem] * (count + 3),
        out_specs=(vmem, vmem),
        scratch_shapes=[
            pltpu.VMEM((count * rows, hidden), jnp.bfloat16),
            pltpu.VMEM((count * rows, LANES), jnp.float32),
        ],
        compiler_params=pltpu.CompilerParams(vmem_limit_bytes=16 * MIB),
        cost_estimate=pl.CostEstimate(
            flops=6 * count * rows * width * hidden * local_count,
            bytes_accessed=6 * width * hidden * local_count,
            transcendentals=count * rows * hidden,
        ),
        name="expert_rows",
    )(*pieces, w_gate, w_up, w_down)


def chip_body(kept, arrived, *outs, dzs, ys):
    rows = outs[0].shape[0]
    for i in range(dzs):
        for j in range(ys):
            at = slice((i * ys + j) * rows, (i * ys + j + 1) * rows)
            out = outs[i * ys + j]
            out[...] = (kept[at] + arrived[at].astype(jnp.float32)).astype(out.dtype)


def chip_sums(kept, arrived, dzs, ys):
    rows, width = kept.shape[0] // (dzs * ys), kept.shape[1]
    vmem = pl.BlockSpec(memory_space=pltpu.VMEM)
    kinds = ([jnp.bfloat16] * (ys - 1) + [jnp.float32]) * dzs
    return pl.pallas_call(
        functools.partial(chip_body, dzs=dzs, ys=ys),
        out_shape=tuple(jax.ShapeDtypeStruct((rows, width), kind) for kind in kinds),
        in_specs=[vmem] * 2,
        out_specs=(vmem,) * len(kinds),
        compiler_params=pltpu.CompilerParams(vmem_limit_bytes=4 * MIB),
        name="chip_sums",
    )(kept, arrived)


def level_body(own, *refs):
    total = own[...]
    for ref in refs[:-1]:
        total = total + ref[...].astype(jnp.float32)
    refs[-1][...] = total.astype(jnp.bfloat16)


def level_sum(own, arrived):
    vmem = pl.BlockSpec(memory_space=pltpu.VMEM)
    return pl.pallas_call(
        level_body,
        out_shape=jax.ShapeDtypeStruct(own.shape, jnp.bfloat16),
        in_specs=[vmem] * (1 + len(arrived)),
        out_specs=vmem,
        compiler_params=pltpu.CompilerParams(vmem_limit_bytes=4 * MIB),
        name="level_sum",
    )(own, *arrived)


def chunks_of(zs):
    order = [zs // 2] + [d for d in range(zs - 1, 0, -1) if d != zs // 2]
    return [[order[0], 0], order[1:]]


def dense(payload, resid, w_gate, w_up, w_down):
    devices = lax.axis_size("ep")
    local_count = w_gate.shape[0]
    experts = devices * local_count
    zs, ys, _ = grid_of(devices)
    f32 = jnp.float32
    pieces = gathered(payload)
    w_down = loaded(payload, w_down)
    w_up = loaded(payload, w_up)
    total = resid
    for chunk in chunks_of(zs):
        dys = list(range(1, ys)) + [0]
        names = [(dz, dy, dc) for dc in (1, 0) for dz in chunk for dy in dys]
        away, kept = expert_rows([pieces[name] for name in names], w_gate, w_up, w_down, experts)
        arrived = send(away, 0, 0, 1)
        sums = chip_sums(kept, arrived, len(chunk), ys)
        for i, dz in enumerate(chunk):
            level = sums[(i + 1) * ys - 1]
            arrived = [send(sums[i * ys + j], 0, dy, 0) for j, dy in enumerate(dys[:-1])]
            if dz:
                level = level_sum(level, arrived)
                arrived = [send(level, dz, 0, 0)]
                total = total + arrived[0].astype(f32)
            else:
                total = total + level
                for part in arrived:
                    total = total + part.astype(f32)
    return total.astype(jnp.bfloat16)


def layer_rows(
    hidden_in,
    queries,
    stored_keys,
    stored_values,
    stored_lengths,
    norm_gain,
    expert_ids,
    gate_weights,
    w_gate,
    w_up,
    w_down,
    capacity,
):
    devices = lax.axis_size("ep")
    experts = devices * w_gate.shape[0]
    if 2 * expert_ids.shape[1] >= experts and dense_fits(devices) and 3 * experts <= LANES:
        payload, resid, w_gate = attention(
            hidden_in, queries, stored_keys, stored_values, stored_lengths, norm_gain,
            expert_ids, gate_weights, w_gate, experts,
        )
        return dense(payload, resid, w_gate, w_up, w_down)
    attention_output = cached_attention(
        queries, stored_keys, stored_values, stored_lengths, QUERY_HEADS, KEY_VALUE_HEADS
    )
    resid = hidden_in.astype(jnp.float32) + attention_output
    mean_square = jnp.mean(resid * resid, axis=-1, keepdims=True)
    normed = (resid * lax.rsqrt(mean_square + 1e-06) * norm_gain[None, :]).astype(jnp.bfloat16)
    mixture = routed(normed, expert_ids, gate_weights, w_gate, w_up, w_down, capacity)
    return (resid + mixture).astype(jnp.bfloat16)


def local(
    hidden_in,
    queries,
    stored_keys,
    stored_values,
    stored_lengths,
    norm_gain,
    expert_ids,
    gate_weights,
    w_gate,
    w_up,
    w_down,
):
    experts = lax.axis_size("ep") * w_gate.shape[0]
    top_count = expert_ids.shape[1]
    capacity = max(2, 3 * MB_ROWS * top_count // (2 * experts))
    return layer_rows(
        hidden_in,
        queries,
        stored_keys,
        stored_values,
        stored_lengths,
        norm_gain,
        expert_ids,
        gate_weights,
        w_gate,
        w_up,
        w_down,
        MB * capacity,
    )


def solution(mesh):
    in_specs = (
        P(("groups", "ep"), None),
        P(("groups", "ep"), None),
        P(("groups", "ep"), None, None),
        P(("groups", "ep"), None, None),
        P(("groups", "ep")),
        P(),
        P(("groups", "ep"), None),
        P(("groups", "ep"), None),
        P("ep", None, None),
        P("ep", None, None),
        P("ep", None, None),
    )
    out_specs = P(("groups", "ep"), None)
    step = jax.shard_map(local, mesh=mesh, in_specs=in_specs, out_specs=out_specs, check_vma=False)
    if not dense_fits(mesh.shape["ep"]):
        return step
    return step
```

```python
import functools
import math

import jax
import jax.numpy as jnp
from jax import lax
from jax.experimental import pallas as pl
from jax.experimental.pallas import tpu as pltpu
from jax.sharding import PartitionSpec as P


QUERY_HEADS = 16
KEY_VALUE_HEADS = 2
MB = 2
MB_ROWS = 16


def cached_attention(queries, stored_keys, stored_values, stored_lengths, heads, kv_heads):
    row_count = queries.shape[0]
    slots = stored_keys.shape[1]
    head_size = queries.shape[1] // heads
    query_head_rows = queries.reshape(row_count, kv_heads, heads // kv_heads, head_size)
    key_head_rows = stored_keys.reshape(row_count, slots, kv_heads, head_size)
    value_head_rows = stored_values.reshape(row_count, slots, kv_heads, head_size)
    scores = jnp.einsum(
        "nkgd,nckd->nkgc", query_head_rows, key_head_rows, preferred_element_type=jnp.float32
    ) / math.sqrt(head_size)
    visible = jnp.arange(slots, dtype=jnp.int32)[None, :] < stored_lengths[:, None]
    visible = visible[:, None, None, :]
    scores = jnp.where(visible, scores, -1e30)
    top_score = jnp.max(scores, axis=-1, keepdims=True)
    expo = jnp.where(visible, jnp.exp(scores - top_score), 0.0)
    probs = (expo / jnp.sum(expo, axis=-1, keepdims=True)).astype(jnp.bfloat16)
    attention_output = jnp.einsum(
        "nkgc,nckd->nkgd", probs, value_head_rows, preferred_element_type=jnp.float32
    )
    return attention_output.reshape(row_count, heads * head_size)


def expert_work(blocks, w_gate, w_up, w_down):
    gate_part = jnp.einsum("secd,edf->secf", blocks, w_gate, preferred_element_type=jnp.float32)
    up_part = jnp.einsum("secd,edf->secf", blocks, w_up, preferred_element_type=jnp.float32)
    inner = (jax.nn.silu(gate_part) * up_part).astype(jnp.bfloat16)
    return jnp.einsum("secf,efd->secd", inner, w_down, preferred_element_type=jnp.float32).astype(
        jnp.bfloat16
    )


def routed(normed, expert_ids, gate_weights, w_gate, w_up, w_down, capacity):
    devices = lax.axis_size("ep")
    local_count = w_gate.shape[0]
    experts = devices * local_count
    width = normed.shape[1]
    row_count, top_count = expert_ids.shape
    flat_ids = expert_ids.reshape(-1)
    onehot_table = (flat_ids[:, None] == jnp.arange(experts, dtype=jnp.int32)[None, :]).astype(
        jnp.int32
    )
    before = jnp.cumsum(onehot_table, axis=0) - onehot_table
    slot_index = jnp.sum(before * onehot_table, axis=1)
    target = flat_ids * capacity + slot_index
    target_rows = target.reshape(row_count, top_count)
    placing = jnp.sum(
        (
            target_rows[:, :, None]
            == jnp.arange(experts * capacity, dtype=jnp.int32)[None, None, :]
        ).astype(jnp.float32),
        axis=1,
    ).astype(jnp.bfloat16)
    buffer = jnp.einsum("tp,td->pd", placing, normed, preferred_element_type=jnp.float32).astype(
        jnp.bfloat16
    )
    buffer = buffer.reshape(experts, capacity, width)
    arrived = lax.all_to_all(buffer, "ep", split_axis=0, concat_axis=0, tiled=True)
    item_count = arrived.shape[1]
    blocks = arrived.reshape(devices, local_count, item_count, width)
    finished = expert_work(blocks, w_gate, w_up, w_down).reshape(experts, item_count, width)
    results = lax.all_to_all(finished, "ep", split_axis=0, concat_axis=0, tiled=True)
    picked = jnp.take(results.reshape(experts * capacity, width), target, axis=0)
    picked = picked.reshape(row_count, top_count, width).astype(jnp.float32)
    return jnp.sum(picked * gate_weights[:, :, None], axis=1)


def grid_of(devices):
    cores = 2 if devices % 2 == 0 else 1
    chips = devices // cores
    minor = max(d for d in range(1, chips + 1) if chips % d == 0 and d * d <= chips)
    return chips // minor, minor, cores


def dense_fits(devices):
    zs, _, cs = grid_of(devices)
    return devices & (devices - 1) == 0 and zs > 2 and cs == 2


def send(x, dz, dy, dc):
    devices = lax.axis_size("ep")
    _, ys, cs = grid_of(devices)
    mask = (dz * ys + dy) * cs + dc
    return lax.ppermute(x, "ep", [(i, i ^ mask) for i in range(devices)])


def near_and_far(zs):
    return list(range(zs // 2)), list(range(zs // 2, zs))


def gathered(x):
    zs, ys, _ = grid_of(lax.axis_size("ep"))
    near, far = near_and_far(zs)
    pieces = {(0, 0): x}
    for dz in near:
        for dy in range(ys):
            if dz or dy:
                pieces[dz, dy] = send(x, dz, dy, 0)
    for dz in far:
        pieces[dz, 0] = send(x, dz, 0, 0)
        for dy in range(1, ys):
            pieces[dz, dy] = send(pieces[dz, 0], 0, dy, 0)
    return pieces


LANES = 128
MIB = 1 << 20


def attention_body(
    lengths_in, hidden_in, queries_in, keys_in, values_in, gain_in, ids_in, gates_in,
    w_gate_in,
    payload, resid, w_gate,
    lengths, hidden, queries, keys, values, gain, ids, gates, parts, sems, *, experts,
):
    rows, width = hidden.shape
    _, slots, kv_width = keys.shape
    head = LANES
    kv_heads = kv_width // head
    heads = width // head
    group = heads // kv_heads
    block = MB_ROWS
    pair = LANES // slots
    scale = 1.0 / math.sqrt(head)
    f32 = jnp.float32

    copies = {}

    def fetch(name, source, target):
        copies[name] = pltpu.make_async_copy(source, target, sems.at[len(copies)])
        copies[name].start()

    fetch("queries", queries_in, queries)
    for b in range(rows // block):
        at = pl.ds(b * block, block)
        fetch(("keys", b), keys_in.at[at], keys.at[at])
        if b == 0:
            fetch("lengths", lengths_in, lengths)
            fetch("ids", ids_in, ids)
            fetch("gates", gates_in, gates)
        fetch(("values", b), values_in.at[at], values.at[at])
        if b == 0:
            fetch("hidden", hidden_in, hidden)
            fetch("gain", gain_in, gain)
    fetch("w_gate", w_gate_in, w_gate)

    copies["ids"].wait()
    copies["gates"].wait()
    number = lax.broadcasted_iota(jnp.int32, (experts, rows), 0)
    table = jnp.zeros((experts, rows), f32)
    for k in range(ids.shape[0]):
        table = table + jnp.where(ids[k : k + 1, :] == number, gates[k : k + 1, :], 0.0)
    high = table.astype(jnp.bfloat16).astype(f32)
    middle = (table - high).astype(jnp.bfloat16).astype(f32)
    low = table - high - middle
    parts[...] = jnp.zeros_like(parts)
    for i, part in enumerate((high, middle, low)):
        parts[i * experts : (i + 1) * experts, :rows] = part
    payload[:, width:] = parts[...].T[:rows].astype(jnp.bfloat16)

    copies["lengths"].wait()
    copies["queries"].wait()
    request = lax.broadcasted_iota(jnp.int32, (block, LANES), 0)
    lane = lax.broadcasted_iota(jnp.int32, (block, LANES), 1)
    slab = jnp.concatenate([request // pair] * heads, axis=0)
    for b in range(rows // block):
        at = slice(b * block, (b + 1) * block)
        blocks = []
        for g in range(kv_heads):
            own = jnp.concatenate(
                [
                    queries[at, h * head : (h + 1) * head]
                    for h in range(g * group, (g + 1) * group)
                ],
                axis=0,
            )
            blank = jnp.zeros_like(own)
            blocks.append(
                jnp.concatenate([own if i == g else blank for i in range(kv_heads)], axis=1)
            )
        stacked = jnp.concatenate(blocks, axis=0)
        copies["keys", b].wait()
        scores = lax.dot_general(
            stacked,
            keys[at].reshape(block * slots, kv_width),
            (((1,), (1,)), ((), ())),
            preferred_element_type=f32,
        )

        length = jnp.zeros((block, LANES), jnp.int32)
        for t in range(block):
            length = jnp.where(request == t, lengths[b * block + t], length)
        seen = (lane // slots == request % pair) & (lane % slots < length)
        seen = jnp.concatenate([seen.astype(jnp.int32)] * heads, axis=0) != 0
        compact = scores[:, :LANES]
        for j in range(1, block // pair):
            compact = jnp.where(slab == j, scores[:, j * LANES : (j + 1) * LANES], compact)
        compact = jnp.where(seen, compact * scale, -1e30)
        top = jnp.max(compact, axis=-1, keepdims=True)
        expo = jnp.where(seen, jnp.exp(compact - top), 0.0)
        probs = (expo / jnp.sum(expo, axis=-1, keepdims=True)).astype(jnp.bfloat16)
        probs = probs.astype(f32)
        wide = jnp.concatenate(
            [jnp.where(slab == j, probs, 0.0).astype(jnp.bfloat16) for j in range(block // pair)],
            axis=1,
        )
        copies["values", b].wait()
        attended = jnp.dot(
            wide, values[at].reshape(block * slots, kv_width), preferred_element_type=f32
        )

        if b == 0:
            copies["hidden"].wait()
            copies["gain"].wait()
        square = jnp.zeros((block, LANES), f32)
        for h in range(heads):
            g = h // group
            cols = slice(h * head, (h + 1) * head)
            total = hidden[at, cols].astype(f32)
            total = total + attended[h * block : (h + 1) * block, g * head : (g + 1) * head]
            resid[at, cols] = total
            square = square + total * total
        mean_square = jnp.sum(square, axis=-1, keepdims=True) / width
        inverse = lax.rsqrt(mean_square + 1e-06)
        for h in range(heads):
            cols = slice(h * head, (h + 1) * head)
            payload[at, cols] = (resid[at, cols] * inverse * gain[:, cols]).astype(jnp.bfloat16)
    copies["w_gate"].wait()


def attention(
    hidden_in, queries, stored_keys, stored_values, stored_lengths, norm_gain, expert_ids,
    gate_weights, w_gate, experts,
):
    rows, width = hidden_in.shape
    whole = width + LANES
    vmem = pl.BlockSpec(memory_space=pltpu.VMEM)
    operands = (
        stored_lengths,
        hidden_in,
        queries,
        stored_keys,
        stored_values,
        norm_gain[None, :],
        expert_ids.T,
        gate_weights.T,
        w_gate,
    )
    return pl.pallas_call(
        functools.partial(attention_body, experts=experts),
        out_shape=(
            jax.ShapeDtypeStruct((rows, whole), jnp.bfloat16),
            jax.ShapeDtypeStruct((rows, width), jnp.float32),
            jax.ShapeDtypeStruct(w_gate.shape, w_gate.dtype),
        ),
        in_specs=[pl.BlockSpec(memory_space=pltpu.HBM)] * len(operands),
        out_specs=(vmem,) * 3,
        scratch_shapes=[
            pltpu.SMEM(operands[0].shape, operands[0].dtype),
            *(pltpu.VMEM(x.shape, x.dtype) for x in operands[1:-1]),
            pltpu.VMEM((LANES, LANES), jnp.float32),
            pltpu.SemaphoreType.DMA((7 + 2 * (rows // MB_ROWS),)),
        ],
        compiler_params=pltpu.CompilerParams(vmem_limit_bytes=16 * MIB),
        name="attention",
    )(*(pltpu.with_memory_space_constraint(x, pltpu.HBM) for x in operands))


def loader_body(after, source, target, sem):
    del after
    copy = pltpu.make_async_copy(source, target, sem)
    copy.start()
    copy.wait()


def loaded(after, x):
    vmem = pl.BlockSpec(memory_space=pltpu.VMEM)
    return pl.pallas_call(
        loader_body,
        out_shape=jax.ShapeDtypeStruct(x.shape, x.dtype),
        in_specs=[vmem, pl.BlockSpec(memory_space=pltpu.HBM)],
        out_specs=vmem,
        scratch_shapes=[pltpu.SemaphoreType.DMA(())],
        compiler_params=pltpu.CompilerParams(vmem_limit_bytes=4 * MIB),
        name="loader",
    )(after, pltpu.with_memory_space_constraint(x, pltpu.HBM))


TILE = 256


def expert_body(*refs, count, experts, local_count):
    pieces, refs = refs[:count], refs[count:]
    sides, outs, (inner, weight) = refs[:6], refs[6:-2], refs[-2:]
    width, hidden = sides[0].shape[1:]
    rows = pieces[0].shape[0]
    f32 = jnp.float32
    filler = [pieces[-1]] * max(0, LANES // rows - count)
    x = jnp.concatenate([piece[:, :width] for piece in (*pieces, *filler)], axis=0)
    table = jnp.concatenate([piece[:, width:] for piece in (*pieces, *filler)], axis=0)
    table = table.astype(f32)
    lane = lax.broadcasted_iota(jnp.int32, table.shape, 1)
    place = lax.axis_index("ep")
    partner = place + 1 - 2 * (place % 2)
    downs = []
    for side, owner in enumerate((place, partner)):
        w_gate, w_up, w_down = sides[3 * side : 3 * side + 3]
        for local in range(local_count):
            expert = owner * local_count + local
            mine = (
                (lane == expert) | (lane == expert + experts) | (lane == expert + 2 * experts)
            )
            slot = len(downs)
            weight[slot] = jnp.broadcast_to(
                jnp.sum(jnp.where(mine, table, 0.0), axis=1, keepdims=True), table.shape
            )
            for f in range(0, hidden, TILE):
                cols = slice(f, f + TILE)
                gate_part = jnp.dot(x, w_gate[local, :, cols], preferred_element_type=f32)
                up_part = jnp.dot(x, w_up[local, :, cols], preferred_element_type=f32)
                silu = gate_part / (1.0 + jnp.exp(-gate_part))
                inner[slot, :, cols] = (silu * up_part).astype(jnp.bfloat16)
            downs.append((w_down, local))
    for d in range(0, width, TILE):
        totals = [0.0] * (TILE // LANES)
        for slot, (w_down, local) in enumerate(downs):
            out = jnp.dot(inner[slot], w_down[local, :, d : d + TILE], preferred_element_type=f32)
            out = out.astype(jnp.bfloat16).astype(f32)
            for j in range(TILE // LANES):
                totals[j] = totals[j] + out[:, j * LANES : (j + 1) * LANES] * weight[slot]
        for j, total in enumerate(totals):
            cols = slice(d + j * LANES, d + (j + 1) * LANES)
            for i, result in enumerate(outs):
                result[:, cols] = total[i * rows : (i + 1) * rows].astype(result.dtype)


def expert_rows(pieces, weights, experts):
    rows = pieces[0].shape[0]
    local_count, width, hidden = weights[0].shape
    count = len(pieces)
    kinds = [jnp.bfloat16] * (count - 1) + [jnp.float32]
    padded = max(count, LANES // rows) * rows
    vmem = pl.BlockSpec(memory_space=pltpu.VMEM)
    return pl.pallas_call(
        functools.partial(
            expert_body, count=count, experts=experts, local_count=local_count
        ),
        out_shape=tuple(jax.ShapeDtypeStruct((rows, width), kind) for kind in kinds),
        in_specs=[vmem] * (count + 6),
        out_specs=(vmem,) * count,
        scratch_shapes=[
            pltpu.VMEM((2 * local_count, padded, hidden), jnp.bfloat16),
            pltpu.VMEM((2 * local_count, padded, LANES), jnp.float32),
        ],
        compiler_params=pltpu.CompilerParams(vmem_limit_bytes=16 * MIB),
        cost_estimate=pl.CostEstimate(
            flops=12 * count * rows * width * hidden * local_count,
            bytes_accessed=12 * width * hidden * local_count,
            transcendentals=2 * count * rows * hidden,
        ),
        name="expert_rows",
    )(*pieces, *weights)


def level_body(own, *refs):
    total = own[...]
    for ref in refs[:-1]:
        total = total + ref[...].astype(jnp.float32)
    refs[-1][...] = total.astype(jnp.bfloat16)


def level_sum(own, arrived):
    vmem = pl.BlockSpec(memory_space=pltpu.VMEM)
    return pl.pallas_call(
        level_body,
        out_shape=jax.ShapeDtypeStruct(own.shape, jnp.bfloat16),
        in_specs=[vmem] * (1 + len(arrived)),
        out_specs=vmem,
        compiler_params=pltpu.CompilerParams(vmem_limit_bytes=4 * MIB),
        name="level_sum",
    )(own, *arrived)


def chunks_of(zs, ys):
    near, far = near_and_far(zs)
    places = [(dz, dy) for dz in near[::-1] for dy in range(ys - 1, -1, -1)]
    return [places] + [[(dz, dy) for dy in range(ys - 1, -1, -1)] for dz in far]


def dense(payload, resid, weights):
    devices = lax.axis_size("ep")
    experts = devices * weights[0].shape[0]
    zs, ys, _ = grid_of(devices)
    pieces = gathered(payload)
    total = resid
    for number, places in enumerate(chunks_of(zs, ys)):
        *leaving, own = expert_rows([pieces[place] for place in places], weights, experts)
        back = [own]
        for (dz, dy), part in zip(places, leaving):
            back.append(send(part, 0 if number else dz, dy, 0))
        if number:
            dz = places[0][0]
            level = level_sum(back[0], back[1:])
            back = [send(level, dz, 0, 0)]
        for part in back:
            total = total + part.astype(jnp.float32)
    return total.astype(jnp.bfloat16)


def layer_rows(
    hidden_in,
    queries,
    stored_keys,
    stored_values,
    stored_lengths,
    norm_gain,
    expert_ids,
    gate_weights,
    w_gate,
    w_up,
    w_down,
    capacity,
):
    devices = lax.axis_size("ep")
    experts = devices * w_gate.shape[0]
    if 2 * expert_ids.shape[1] >= experts and dense_fits(devices) and 3 * experts <= LANES:
        other = [send(w, 0, 0, 1) for w in (w_gate, w_up, w_down)]
        payload, resid, w_gate = attention(
            hidden_in, queries, stored_keys, stored_values, stored_lengths, norm_gain,
            expert_ids, gate_weights, w_gate, experts,
        )
        w_down = loaded(payload, w_down)
        w_up = loaded(payload, w_up)
        return dense(payload, resid, (w_gate, w_up, w_down, *other))
    attention_output = cached_attention(
        queries, stored_keys, stored_values, stored_lengths, QUERY_HEADS, KEY_VALUE_HEADS
    )
    resid = hidden_in.astype(jnp.float32) + attention_output
    mean_square = jnp.mean(resid * resid, axis=-1, keepdims=True)
    normed = (resid * lax.rsqrt(mean_square + 1e-06) * norm_gain[None, :]).astype(jnp.bfloat16)
    mixture = routed(normed, expert_ids, gate_weights, w_gate, w_up, w_down, capacity)
    return (resid + mixture).astype(jnp.bfloat16)


def local(
    hidden_in,
    queries,
    stored_keys,
    stored_values,
    stored_lengths,
    norm_gain,
    expert_ids,
    gate_weights,
    w_gate,
    w_up,
    w_down,
):
    experts = lax.axis_size("ep") * w_gate.shape[0]
    top_count = expert_ids.shape[1]
    capacity = max(2, 3 * MB_ROWS * top_count // (2 * experts))
    return layer_rows(
        hidden_in,
        queries,
        stored_keys,
        stored_values,
        stored_lengths,
        norm_gain,
        expert_ids,
        gate_weights,
        w_gate,
        w_up,
        w_down,
        MB * capacity,
    )


def solution(mesh):
    in_specs = (
        P(("groups", "ep"), None),
        P(("groups", "ep"), None),
        P(("groups", "ep"), None, None),
        P(("groups", "ep"), None, None),
        P(("groups", "ep")),
        P(),
        P(("groups", "ep"), None),
        P(("groups", "ep"), None),
        P("ep", None, None),
        P("ep", None, None),
        P("ep", None, None),
    )
    out_specs = P(("groups", "ep"), None)
    step = jax.shard_map(local, mesh=mesh, in_specs=in_specs, out_specs=out_specs, check_vma=False)
    if not dense_fits(mesh.shape["ep"]):
        return step
    return step
```

```python
import functools
import math

import jax
import jax.numpy as jnp
from jax import lax
from jax.experimental import pallas as pl
from jax.experimental.pallas import tpu as pltpu
from jax.sharding import PartitionSpec as P


QUERY_HEADS = 16
KEY_VALUE_HEADS = 2
MB = 2
MB_ROWS = 16


def cached_attention(queries, stored_keys, stored_values, stored_lengths, heads, kv_heads):
    row_count = queries.shape[0]
    slots = stored_keys.shape[1]
    head_size = queries.shape[1] // heads
    query_head_rows = queries.reshape(row_count, kv_heads, heads // kv_heads, head_size)
    key_head_rows = stored_keys.reshape(row_count, slots, kv_heads, head_size)
    value_head_rows = stored_values.reshape(row_count, slots, kv_heads, head_size)
    scores = jnp.einsum(
        "nkgd,nckd->nkgc", query_head_rows, key_head_rows, preferred_element_type=jnp.float32
    ) / math.sqrt(head_size)
    visible = jnp.arange(slots, dtype=jnp.int32)[None, :] < stored_lengths[:, None]
    visible = visible[:, None, None, :]
    scores = jnp.where(visible, scores, -1e30)
    top_score = jnp.max(scores, axis=-1, keepdims=True)
    expo = jnp.where(visible, jnp.exp(scores - top_score), 0.0)
    probs = (expo / jnp.sum(expo, axis=-1, keepdims=True)).astype(jnp.bfloat16)
    attention_output = jnp.einsum(
        "nkgc,nckd->nkgd", probs, value_head_rows, preferred_element_type=jnp.float32
    )
    return attention_output.reshape(row_count, heads * head_size)


def expert_work(blocks, w_gate, w_up, w_down):
    gate_part = jnp.einsum("secd,edf->secf", blocks, w_gate, preferred_element_type=jnp.float32)
    up_part = jnp.einsum("secd,edf->secf", blocks, w_up, preferred_element_type=jnp.float32)
    inner = (jax.nn.silu(gate_part) * up_part).astype(jnp.bfloat16)
    return jnp.einsum("secf,efd->secd", inner, w_down, preferred_element_type=jnp.float32).astype(
        jnp.bfloat16
    )


def routed(normed, expert_ids, gate_weights, w_gate, w_up, w_down, capacity):
    devices = lax.axis_size("ep")
    local_count = w_gate.shape[0]
    experts = devices * local_count
    width = normed.shape[1]
    row_count, top_count = expert_ids.shape
    flat_ids = expert_ids.reshape(-1)
    onehot_table = (flat_ids[:, None] == jnp.arange(experts, dtype=jnp.int32)[None, :]).astype(
        jnp.int32
    )
    before = jnp.cumsum(onehot_table, axis=0) - onehot_table
    slot_index = jnp.sum(before * onehot_table, axis=1)
    target = flat_ids * capacity + slot_index
    target_rows = target.reshape(row_count, top_count)
    placing = jnp.sum(
        (
            target_rows[:, :, None]
            == jnp.arange(experts * capacity, dtype=jnp.int32)[None, None, :]
        ).astype(jnp.float32),
        axis=1,
    ).astype(jnp.bfloat16)
    buffer = jnp.einsum("tp,td->pd", placing, normed, preferred_element_type=jnp.float32).astype(
        jnp.bfloat16
    )
    buffer = buffer.reshape(experts, capacity, width)
    arrived = lax.all_to_all(buffer, "ep", split_axis=0, concat_axis=0, tiled=True)
    item_count = arrived.shape[1]
    blocks = arrived.reshape(devices, local_count, item_count, width)
    finished = expert_work(blocks, w_gate, w_up, w_down).reshape(experts, item_count, width)
    results = lax.all_to_all(finished, "ep", split_axis=0, concat_axis=0, tiled=True)
    picked = jnp.take(results.reshape(experts * capacity, width), target, axis=0)
    picked = picked.reshape(row_count, top_count, width).astype(jnp.float32)
    return jnp.sum(picked * gate_weights[:, :, None], axis=1)


def grid_of(devices):
    cores = 2 if devices % 2 == 0 else 1
    chips = devices // cores
    minor = max(d for d in range(1, chips + 1) if chips % d == 0 and d * d <= chips)
    return chips // minor, minor, cores


def dense_fits(devices):
    zs, _, cs = grid_of(devices)
    return devices & (devices - 1) == 0 and zs > 2 and cs == 2


def send(x, dz, dy, dc):
    devices = lax.axis_size("ep")
    _, ys, cs = grid_of(devices)
    mask = (dz * ys + dy) * cs + dc
    return lax.ppermute(x, "ep", [(i, i ^ mask) for i in range(devices)])


def near_and_far(zs):
    return list(range(zs // 2)), list(range(zs // 2, zs))


def gathered(x):
    zs, ys, _ = grid_of(lax.axis_size("ep"))
    near, far = near_and_far(zs)
    pieces = {(0, 0): x}
    for dz in near:
        for dy in range(ys):
            if dz or dy:
                pieces[dz, dy] = send(x, dz, dy, 0)
    for dz in far:
        pieces[dz, 0] = send(x, dz, 0, 0)
        for dy in range(1, ys):
            pieces[dz, dy] = send(pieces[dz, 0], 0, dy, 0)
    return pieces


LANES = 128
MIB = 1 << 20


def attention_body(
    lengths_in, hidden_in, queries_in, keys_in, values_in, gain_in, ids_in, gates_in,
    w_gate_in,
    payload, resid, w_gate,
    lengths, hidden, queries, keys, values, gain, ids, gates, parts, sems, *, experts,
):
    rows, width = hidden.shape
    _, slots, kv_width = keys.shape
    head = LANES
    kv_heads = kv_width // head
    heads = width // head
    group = heads // kv_heads
    block = MB_ROWS
    pair = LANES // slots
    scale = 1.0 / math.sqrt(head)
    f32 = jnp.float32

    copies = {}

    def fetch(name, source, target):
        copies[name] = pltpu.make_async_copy(source, target, sems.at[len(copies)])
        copies[name].start()

    fetch("queries", queries_in, queries)
    for b in range(rows // block):
        at = pl.ds(b * block, block)
        fetch(("keys", b), keys_in.at[at], keys.at[at])
        if b == 0:
            fetch("lengths", lengths_in, lengths)
            fetch("ids", ids_in, ids)
            fetch("gates", gates_in, gates)
        fetch(("values", b), values_in.at[at], values.at[at])
        if b == 0:
            fetch("hidden", hidden_in, hidden)
            fetch("gain", gain_in, gain)
    fetch("w_gate", w_gate_in, w_gate)

    copies["ids"].wait()
    copies["gates"].wait()
    number = lax.broadcasted_iota(jnp.int32, (experts, rows), 0)
    table = jnp.zeros((experts, rows), f32)
    for k in range(ids.shape[0]):
        table = table + jnp.where(ids[k : k + 1, :] == number, gates[k : k + 1, :], 0.0)
    high = table.astype(jnp.bfloat16).astype(f32)
    middle = (table - high).astype(jnp.bfloat16).astype(f32)
    low = table - high - middle
    parts[...] = jnp.zeros_like(parts)
    for i, part in enumerate((high, middle, low)):
        parts[i * experts : (i + 1) * experts, :rows] = part
    payload[:, width:] = parts[...].T[:rows].astype(jnp.bfloat16)

    copies["lengths"].wait()
    copies["queries"].wait()
    request = lax.broadcasted_iota(jnp.int32, (block, LANES), 0)
    lane = lax.broadcasted_iota(jnp.int32, (block, LANES), 1)
    slab = jnp.concatenate([request // pair] * heads, axis=0)
    for b in range(rows // block):
        at = slice(b * block, (b + 1) * block)
        blocks = []
        for g in range(kv_heads):
            own = jnp.concatenate(
                [
                    queries[at, h * head : (h + 1) * head]
                    for h in range(g * group, (g + 1) * group)
                ],
                axis=0,
            )
            blank = jnp.zeros_like(own)
            blocks.append(
                jnp.concatenate([own if i == g else blank for i in range(kv_heads)], axis=1)
            )
        stacked = jnp.concatenate(blocks, axis=0)
        copies["keys", b].wait()
        scores = lax.dot_general(
            stacked,
            keys[at].reshape(block * slots, kv_width),
            (((1,), (1,)), ((), ())),
            preferred_element_type=f32,
        )

        length = jnp.zeros((block, LANES), jnp.int32)
        for t in range(block):
            length = jnp.where(request == t, lengths[b * block + t], length)
        seen = (lane // slots == request % pair) & (lane % slots < length)
        seen = jnp.concatenate([seen.astype(jnp.int32)] * heads, axis=0) != 0
        compact = scores[:, :LANES]
        for j in range(1, block // pair):
            compact = jnp.where(slab == j, scores[:, j * LANES : (j + 1) * LANES], compact)
        compact = jnp.where(seen, compact * scale, -1e30)
        top = jnp.max(compact, axis=-1, keepdims=True)
        expo = jnp.where(seen, jnp.exp(compact - top), 0.0)
        probs = (expo / jnp.sum(expo, axis=-1, keepdims=True)).astype(jnp.bfloat16)
        probs = probs.astype(f32)
        wide = jnp.concatenate(
            [jnp.where(slab == j, probs, 0.0).astype(jnp.bfloat16) for j in range(block // pair)],
            axis=1,
        )
        copies["values", b].wait()
        attended = jnp.dot(
            wide, values[at].reshape(block * slots, kv_width), preferred_element_type=f32
        )

        if b == 0:
            copies["hidden"].wait()
            copies["gain"].wait()
        square = jnp.zeros((block, LANES), f32)
        for h in range(heads):
            g = h // group
            cols = slice(h * head, (h + 1) * head)
            total = hidden[at, cols].astype(f32)
            total = total + attended[h * block : (h + 1) * block, g * head : (g + 1) * head]
            resid[at, cols] = total
            square = square + total * total
        mean_square = jnp.sum(square, axis=-1, keepdims=True) / width
        inverse = lax.rsqrt(mean_square + 1e-06)
        for h in range(heads):
            cols = slice(h * head, (h + 1) * head)
            payload[at, cols] = (resid[at, cols] * inverse * gain[:, cols]).astype(jnp.bfloat16)
    copies["w_gate"].wait()


def attention(
    hidden_in, queries, stored_keys, stored_values, stored_lengths, norm_gain, expert_ids,
    gate_weights, w_gate, experts,
):
    rows, width = hidden_in.shape
    whole = width + LANES
    vmem = pl.BlockSpec(memory_space=pltpu.VMEM)
    operands = (
        stored_lengths,
        hidden_in,
        queries,
        stored_keys,
        stored_values,
        norm_gain[None, :],
        expert_ids.T,
        gate_weights.T,
        w_gate,
    )
    return pl.pallas_call(
        functools.partial(attention_body, experts=experts),
        out_shape=(
            jax.ShapeDtypeStruct((rows, whole), jnp.bfloat16),
            jax.ShapeDtypeStruct((rows, width), jnp.float32),
            jax.ShapeDtypeStruct(w_gate.shape, w_gate.dtype),
        ),
        in_specs=[pl.BlockSpec(memory_space=pltpu.HBM)] * len(operands),
        out_specs=(vmem,) * 3,
        scratch_shapes=[
            pltpu.SMEM(operands[0].shape, operands[0].dtype),
            *(pltpu.VMEM(x.shape, x.dtype) for x in operands[1:-1]),
            pltpu.VMEM((LANES, LANES), jnp.float32),
            pltpu.SemaphoreType.DMA((7 + 2 * (rows // MB_ROWS),)),
        ],
        compiler_params=pltpu.CompilerParams(vmem_limit_bytes=16 * MIB),
        name="attention",
    )(*(pltpu.with_memory_space_constraint(x, pltpu.HBM) for x in operands))


def loader_body(after, source, target, sem):
    del after
    copy = pltpu.make_async_copy(source, target, sem)
    copy.start()
    copy.wait()


def loaded(after, x):
    vmem = pl.BlockSpec(memory_space=pltpu.VMEM)
    return pl.pallas_call(
        loader_body,
        out_shape=jax.ShapeDtypeStruct(x.shape, x.dtype),
        in_specs=[vmem, pl.BlockSpec(memory_space=pltpu.HBM)],
        out_specs=vmem,
        scratch_shapes=[pltpu.SemaphoreType.DMA(())],
        compiler_params=pltpu.CompilerParams(vmem_limit_bytes=4 * MIB),
        name="loader",
    )(after, pltpu.with_memory_space_constraint(x, pltpu.HBM))


TILE = 256


def expert_body(*refs, count, experts, local_count):
    pieces, refs = refs[:count], refs[count:]
    sides, outs, (inner, weight) = refs[:6], refs[6:-2], refs[-2:]
    width, hidden = sides[0].shape[1:]
    rows = pieces[0].shape[0]
    f32 = jnp.float32
    filler = [pieces[-1]] * max(0, LANES // rows - count)
    x = jnp.concatenate([piece[:, :width] for piece in (*pieces, *filler)], axis=0)
    table = jnp.concatenate([piece[:, width:] for piece in (*pieces, *filler)], axis=0)
    table = table.astype(f32)
    lane = lax.broadcasted_iota(jnp.int32, table.shape, 1)
    place = lax.axis_index("ep")
    partner = place + 1 - 2 * (place % 2)
    downs = []
    for side, owner in enumerate((place, partner)):
        w_gate, w_up, w_down = sides[3 * side : 3 * side + 3]
        for local in range(local_count):
            expert = owner * local_count + local
            mine = (
                (lane == expert) | (lane == expert + experts) | (lane == expert + 2 * experts)
            )
            slot = len(downs)
            weight[slot] = jnp.broadcast_to(
                jnp.sum(jnp.where(mine, table, 0.0), axis=1, keepdims=True), table.shape
            )
            for f in range(0, hidden, TILE):
                cols = slice(f, f + TILE)
                gate_part = jnp.dot(x, w_gate[local, :, cols], preferred_element_type=f32)
                up_part = jnp.dot(x, w_up[local, :, cols], preferred_element_type=f32)
                silu = gate_part / (1.0 + jnp.exp(-gate_part))
                inner[slot, :, cols] = (silu * up_part).astype(jnp.bfloat16)
            downs.append((w_down, local))
    for d in range(0, width, TILE):
        totals = [0.0] * (TILE // LANES)
        for slot, (w_down, local) in enumerate(downs):
            out = jnp.dot(inner[slot], w_down[local, :, d : d + TILE], preferred_element_type=f32)
            out = out.astype(jnp.bfloat16).astype(f32)
            for j in range(TILE // LANES):
                totals[j] = totals[j] + out[:, j * LANES : (j + 1) * LANES] * weight[slot]
        for j, total in enumerate(totals):
            cols = slice(d + j * LANES, d + (j + 1) * LANES)
            for i, result in enumerate(outs):
                result[:, cols] = total[i * rows : (i + 1) * rows].astype(result.dtype)


def expert_rows(pieces, weights, experts, kinds):
    rows = pieces[0].shape[0]
    local_count, width, hidden = weights[0].shape
    count = len(pieces)
    padded = max(count, LANES // rows) * rows
    vmem = pl.BlockSpec(memory_space=pltpu.VMEM)
    return pl.pallas_call(
        functools.partial(
            expert_body, count=count, experts=experts, local_count=local_count
        ),
        out_shape=tuple(jax.ShapeDtypeStruct((rows, width), kind) for kind in kinds),
        in_specs=[vmem] * (count + 6),
        out_specs=(vmem,) * count,
        scratch_shapes=[
            pltpu.VMEM((2 * local_count, padded, hidden), jnp.bfloat16),
            pltpu.VMEM((2 * local_count, padded, LANES), jnp.float32),
        ],
        compiler_params=pltpu.CompilerParams(vmem_limit_bytes=16 * MIB),
        cost_estimate=pl.CostEstimate(
            flops=12 * count * rows * width * hidden * local_count,
            bytes_accessed=12 * width * hidden * local_count,
            transcendentals=2 * count * rows * hidden,
        ),
        name="expert_rows",
    )(*pieces, *weights)


def level_body(own, *refs):
    total = own[...]
    for ref in refs[:-1]:
        total = total + ref[...].astype(jnp.float32)
    refs[-1][...] = total.astype(jnp.bfloat16)


def level_sum(own, arrived):
    vmem = pl.BlockSpec(memory_space=pltpu.VMEM)
    return pl.pallas_call(
        level_body,
        out_shape=jax.ShapeDtypeStruct(own.shape, jnp.bfloat16),
        in_specs=[vmem] * (1 + len(arrived)),
        out_specs=vmem,
        compiler_params=pltpu.CompilerParams(vmem_limit_bytes=4 * MIB),
        name="level_sum",
    )(own, *arrived)


def chunks_of(zs, ys):
    near, far = near_and_far(zs)
    return [[(dz, dy) for dy in range(ys) for dz in pair] for pair in zip(far, near)]


def dense(payload, resid, weights):
    devices = lax.axis_size("ep")
    experts = devices * weights[0].shape[0]
    zs, ys, _ = grid_of(devices)
    far = near_and_far(zs)[1]
    pieces = gathered(payload)
    total = resid
    for number, places in enumerate(chunks_of(zs, ys)):
        here = [(far[number], 0), (0, 0)]
        kinds = [jnp.float32 if place in here else jnp.bfloat16 for place in places]
        sums = expert_rows([pieces[place] for place in places], weights, experts, kinds)
        sums = dict(zip(places, sums))
        arrived = []
        for (dz, dy), part in sums.items():
            if dz == far[number]:
                arrived += [send(part, 0, dy, 0)] if dy else []
            else:
                back = send(part, dz, dy, 0) if dz or dy else part
                total = total + back.astype(jnp.float32)
        level = level_sum(sums[far[number], 0], arrived)
        back = send(level, far[number], 0, 0)
        total = total + back.astype(jnp.float32)
    return total.astype(jnp.bfloat16)


def layer_rows(
    hidden_in,
    queries,
    stored_keys,
    stored_values,
    stored_lengths,
    norm_gain,
    expert_ids,
    gate_weights,
    w_gate,
    w_up,
    w_down,
    capacity,
):
    devices = lax.axis_size("ep")
    experts = devices * w_gate.shape[0]
    if 2 * expert_ids.shape[1] >= experts and dense_fits(devices) and 3 * experts <= LANES:
        other = [send(w, 0, 0, 1) for w in (w_gate, w_up, w_down)]
        payload, resid, w_gate = attention(
            hidden_in, queries, stored_keys, stored_values, stored_lengths, norm_gain,
            expert_ids, gate_weights, w_gate, experts,
        )
        w_down = loaded(payload, w_down)
        w_up = loaded(payload, w_up)
        return dense(payload, resid, (w_gate, w_up, w_down, *other))
    attention_output = cached_attention(
        queries, stored_keys, stored_values, stored_lengths, QUERY_HEADS, KEY_VALUE_HEADS
    )
    resid = hidden_in.astype(jnp.float32) + attention_output
    mean_square = jnp.mean(resid * resid, axis=-1, keepdims=True)
    normed = (resid * lax.rsqrt(mean_square + 1e-06) * norm_gain[None, :]).astype(jnp.bfloat16)
    mixture = routed(normed, expert_ids, gate_weights, w_gate, w_up, w_down, capacity)
    return (resid + mixture).astype(jnp.bfloat16)


def local(
    hidden_in,
    queries,
    stored_keys,
    stored_values,
    stored_lengths,
    norm_gain,
    expert_ids,
    gate_weights,
    w_gate,
    w_up,
    w_down,
):
    experts = lax.axis_size("ep") * w_gate.shape[0]
    top_count = expert_ids.shape[1]
    capacity = max(2, 3 * MB_ROWS * top_count // (2 * experts))
    return layer_rows(
        hidden_in,
        queries,
        stored_keys,
        stored_values,
        stored_lengths,
        norm_gain,
        expert_ids,
        gate_weights,
        w_gate,
        w_up,
        w_down,
        MB * capacity,
    )


def solution(mesh):
    in_specs = (
        P(("groups", "ep"), None),
        P(("groups", "ep"), None),
        P(("groups", "ep"), None, None),
        P(("groups", "ep"), None, None),
        P(("groups", "ep")),
        P(),
        P(("groups", "ep"), None),
        P(("groups", "ep"), None),
        P("ep", None, None),
        P("ep", None, None),
        P("ep", None, None),
    )
    out_specs = P(("groups", "ep"), None)
    step = jax.shard_map(local, mesh=mesh, in_specs=in_specs, out_specs=out_specs, check_vma=False)
    if not dense_fits(mesh.shape["ep"]):
        return step
    return step
```

```python
import functools
import math

import jax
import jax.numpy as jnp
from jax import lax
from jax.experimental import pallas as pl
from jax.experimental.pallas import tpu as pltpu
from jax.sharding import PartitionSpec as P


QUERY_HEADS = 16
KEY_VALUE_HEADS = 2
MB = 2
MB_ROWS = 16


def cached_attention(queries, stored_keys, stored_values, stored_lengths, heads, kv_heads):
    row_count = queries.shape[0]
    slots = stored_keys.shape[1]
    head_size = queries.shape[1] // heads
    query_head_rows = queries.reshape(row_count, kv_heads, heads // kv_heads, head_size)
    key_head_rows = stored_keys.reshape(row_count, slots, kv_heads, head_size)
    value_head_rows = stored_values.reshape(row_count, slots, kv_heads, head_size)
    scores = jnp.einsum(
        "nkgd,nckd->nkgc", query_head_rows, key_head_rows, preferred_element_type=jnp.float32
    ) / math.sqrt(head_size)
    visible = jnp.arange(slots, dtype=jnp.int32)[None, :] < stored_lengths[:, None]
    visible = visible[:, None, None, :]
    scores = jnp.where(visible, scores, -1e30)
    top_score = jnp.max(scores, axis=-1, keepdims=True)
    expo = jnp.where(visible, jnp.exp(scores - top_score), 0.0)
    probs = (expo / jnp.sum(expo, axis=-1, keepdims=True)).astype(jnp.bfloat16)
    attention_output = jnp.einsum(
        "nkgc,nckd->nkgd", probs, value_head_rows, preferred_element_type=jnp.float32
    )
    return attention_output.reshape(row_count, heads * head_size)


def expert_work(blocks, w_gate, w_up, w_down):
    gate_part = jnp.einsum("secd,edf->secf", blocks, w_gate, preferred_element_type=jnp.float32)
    up_part = jnp.einsum("secd,edf->secf", blocks, w_up, preferred_element_type=jnp.float32)
    inner = (jax.nn.silu(gate_part) * up_part).astype(jnp.bfloat16)
    return jnp.einsum("secf,efd->secd", inner, w_down, preferred_element_type=jnp.float32).astype(
        jnp.bfloat16
    )


def routed(normed, expert_ids, gate_weights, w_gate, w_up, w_down, capacity):
    devices = lax.axis_size("ep")
    local_count = w_gate.shape[0]
    experts = devices * local_count
    width = normed.shape[1]
    row_count, top_count = expert_ids.shape
    flat_ids = expert_ids.reshape(-1)
    onehot_table = (flat_ids[:, None] == jnp.arange(experts, dtype=jnp.int32)[None, :]).astype(
        jnp.int32
    )
    before = jnp.cumsum(onehot_table, axis=0) - onehot_table
    slot_index = jnp.sum(before * onehot_table, axis=1)
    target = flat_ids * capacity + slot_index
    target_rows = target.reshape(row_count, top_count)
    placing = jnp.sum(
        (
            target_rows[:, :, None]
            == jnp.arange(experts * capacity, dtype=jnp.int32)[None, None, :]
        ).astype(jnp.float32),
        axis=1,
    ).astype(jnp.bfloat16)
    buffer = jnp.einsum("tp,td->pd", placing, normed, preferred_element_type=jnp.float32).astype(
        jnp.bfloat16
    )
    buffer = buffer.reshape(experts, capacity, width)
    arrived = lax.all_to_all(buffer, "ep", split_axis=0, concat_axis=0, tiled=True)
    item_count = arrived.shape[1]
    blocks = arrived.reshape(devices, local_count, item_count, width)
    finished = expert_work(blocks, w_gate, w_up, w_down).reshape(experts, item_count, width)
    results = lax.all_to_all(finished, "ep", split_axis=0, concat_axis=0, tiled=True)
    picked = jnp.take(results.reshape(experts * capacity, width), target, axis=0)
    picked = picked.reshape(row_count, top_count, width).astype(jnp.float32)
    return jnp.sum(picked * gate_weights[:, :, None], axis=1)


def grid_of(devices):
    cores = 2 if devices % 2 == 0 else 1
    chips = devices // cores
    minor = max(d for d in range(1, chips + 1) if chips % d == 0 and d * d <= chips)
    return chips // minor, minor, cores


def dense_fits(devices):
    zs, _, cs = grid_of(devices)
    return devices & (devices - 1) == 0 and zs == 4 and cs == 2


def send(x, dz, dy, dc):
    devices = lax.axis_size("ep")
    _, ys, cs = grid_of(devices)
    mask = (dz * ys + dy) * cs + dc
    return lax.ppermute(x, "ep", [(i, i ^ mask) for i in range(devices)])


def far_levels(zs):
    return list(range(zs // 2, zs))


def gathered(x):
    zs, ys, _ = grid_of(lax.axis_size("ep"))
    pieces = {(0, 0): x}
    for dz in range(zs // 2):
        for dy in range(ys):
            if dz or dy:
                pieces[dz, dy] = send(x, dz, dy, 0)
    for dz in far_levels(zs):
        pieces[dz, 0] = send(x, dz, 0, 0)
        for dy in range(1, ys):
            pieces[dz, dy] = send(pieces[dz, 0], 0, dy, 0)
    return pieces


LANES = 128
MIB = 1 << 20


def attention_body(
    lengths_in, hidden_in, queries_in, keys_in, values_in, gain_in, ids_in, gates_in,
    w_gate_in,
    payload, resid, w_gate,
    lengths, hidden, queries, keys, values, gain, ids, gates, parts, sems, *, experts,
):
    rows, width = hidden.shape
    _, slots, kv_width = keys.shape
    head = LANES
    kv_heads = kv_width // head
    heads = width // head
    group = heads // kv_heads
    block = MB_ROWS
    pair = LANES // slots
    scale = 1.0 / math.sqrt(head)
    f32 = jnp.float32

    copies = {}

    def fetch(name, source, target):
        copies[name] = pltpu.make_async_copy(source, target, sems.at[len(copies)])
        copies[name].start()

    fetch("ids", ids_in, ids)
    fetch("gates", gates_in, gates)
    fetch("queries", queries_in, queries)
    for b in range(rows // block):
        at = pl.ds(b * block, block)
        fetch(("keys", b), keys_in.at[at], keys.at[at])
        if b == 0:
            fetch("lengths", lengths_in, lengths)
        fetch(("values", b), values_in.at[at], values.at[at])
        if b == 0:
            fetch("hidden", hidden_in, hidden)
            fetch("gain", gain_in, gain)
    fetch("w_gate", w_gate_in, w_gate)

    copies["ids"].wait()
    copies["gates"].wait()
    number = lax.broadcasted_iota(jnp.int32, (experts, rows), 0)
    table = jnp.zeros((experts, rows), f32)
    for k in range(ids.shape[0]):
        table = table + jnp.where(ids[k : k + 1, :] == number, gates[k : k + 1, :], 0.0)
    high = table.astype(jnp.bfloat16).astype(f32)
    middle = (table - high).astype(jnp.bfloat16).astype(f32)
    low = table - high - middle
    parts[...] = jnp.zeros_like(parts)
    for i, part in enumerate((high, middle, low)):
        parts[i * experts : (i + 1) * experts, :rows] = part
    payload[:, width:] = parts[...].T[:rows].astype(jnp.bfloat16)

    copies["lengths"].wait()
    copies["queries"].wait()
    request = lax.broadcasted_iota(jnp.int32, (block, LANES), 0)
    lane = lax.broadcasted_iota(jnp.int32, (block, LANES), 1)
    slab = jnp.concatenate([request // pair] * heads, axis=0)
    spread = []
    for b in range(rows // block):
        at = slice(b * block, (b + 1) * block)
        blocks = []
        for g in range(kv_heads):
            own = jnp.concatenate(
                [
                    queries[at, h * head : (h + 1) * head]
                    for h in range(g * group, (g + 1) * group)
                ],
                axis=0,
            )
            blank = jnp.zeros_like(own)
            blocks.append(
                jnp.concatenate([own if i == g else blank for i in range(kv_heads)], axis=1)
            )
        stacked = jnp.concatenate(blocks, axis=0)
        copies["keys", b].wait()
        scores = lax.dot_general(
            stacked,
            keys[at].reshape(block * slots, kv_width),
            (((1,), (1,)), ((), ())),
            preferred_element_type=f32,
        )

        length = jnp.zeros((block, LANES), jnp.int32)
        for t in range(block):
            length = jnp.where(request == t, lengths[b * block + t], length)
        seen = (lane // slots == request % pair) & (lane % slots < length)
        seen = jnp.concatenate([seen.astype(jnp.int32)] * heads, axis=0) != 0
        compact = scores[:, :LANES]
        for j in range(1, block // pair):
            compact = jnp.where(slab == j, scores[:, j * LANES : (j + 1) * LANES], compact)
        compact = jnp.where(seen, compact * scale, -1e30)
        top = jnp.max(compact, axis=-1, keepdims=True)
        expo = jnp.where(seen, jnp.exp(compact - top), 0.0)
        probs = (expo / jnp.sum(expo, axis=-1, keepdims=True)).astype(jnp.bfloat16)
        probs = probs.astype(f32)
        wide = jnp.concatenate(
            [jnp.where(slab == j, probs, 0.0).astype(jnp.bfloat16) for j in range(block // pair)],
            axis=1,
        )
        spread.append(wide)
    for b, wide in enumerate(spread):
        at = slice(b * block, (b + 1) * block)
        copies["values", b].wait()
        attended = jnp.dot(
            wide, values[at].reshape(block * slots, kv_width), preferred_element_type=f32
        )

        if b == 0:
            copies["hidden"].wait()
            copies["gain"].wait()
        square = jnp.zeros((block, LANES), f32)
        for h in range(heads):
            g = h // group
            cols = slice(h * head, (h + 1) * head)
            total = hidden[at, cols].astype(f32)
            total = total + attended[h * block : (h + 1) * block, g * head : (g + 1) * head]
            resid[at, cols] = total
            square = square + total * total
        mean_square = jnp.sum(square, axis=-1, keepdims=True) / width
        inverse = lax.rsqrt(mean_square + 1e-06)
        for h in range(heads):
            cols = slice(h * head, (h + 1) * head)
            payload[at, cols] = (resid[at, cols] * inverse * gain[:, cols]).astype(jnp.bfloat16)
    copies["w_gate"].wait()


def attention(
    hidden_in, queries, stored_keys, stored_values, stored_lengths, norm_gain, expert_ids,
    gate_weights, w_gate, experts,
):
    rows, width = hidden_in.shape
    whole = width + LANES
    vmem = pl.BlockSpec(memory_space=pltpu.VMEM)
    operands = (
        stored_lengths,
        hidden_in,
        queries,
        stored_keys,
        stored_values,
        norm_gain[None, :],
        expert_ids.T,
        gate_weights.T,
        w_gate,
    )
    return pl.pallas_call(
        functools.partial(attention_body, experts=experts),
        out_shape=(
            jax.ShapeDtypeStruct((rows, whole), jnp.bfloat16),
            jax.ShapeDtypeStruct((rows, width), jnp.float32),
            jax.ShapeDtypeStruct(w_gate.shape, w_gate.dtype),
        ),
        in_specs=[pl.BlockSpec(memory_space=pltpu.HBM)] * len(operands),
        out_specs=(vmem,) * 3,
        scratch_shapes=[
            pltpu.SMEM(operands[0].shape, operands[0].dtype),
            *(pltpu.VMEM(x.shape, x.dtype) for x in operands[1:-1]),
            pltpu.VMEM((LANES, LANES), jnp.float32),
            pltpu.SemaphoreType.DMA((7 + 2 * (rows // MB_ROWS),)),
        ],
        compiler_params=pltpu.CompilerParams(vmem_limit_bytes=16 * MIB),
        name="attention",
    )(*(pltpu.with_memory_space_constraint(x, pltpu.HBM) for x in operands))


def loader_body(after, source, target, sem):
    del after
    copy = pltpu.make_async_copy(source, target, sem)
    copy.start()
    copy.wait()


def loaded(after, x):
    vmem = pl.BlockSpec(memory_space=pltpu.VMEM)
    return pl.pallas_call(
        loader_body,
        out_shape=jax.ShapeDtypeStruct(x.shape, x.dtype),
        in_specs=[vmem, pl.BlockSpec(memory_space=pltpu.HBM)],
        out_specs=vmem,
        scratch_shapes=[pltpu.SemaphoreType.DMA(())],
        compiler_params=pltpu.CompilerParams(vmem_limit_bytes=4 * MIB),
        name="loader",
    )(after, pltpu.with_memory_space_constraint(x, pltpu.HBM))


TILE = 256


def expert_body(*refs, count, experts, local_count):
    pieces, refs = refs[:count], refs[count:]
    sides, outs, (inner, weight) = refs[:6], refs[6:-2], refs[-2:]
    width, hidden = sides[0].shape[1:]
    f32 = jnp.float32
    x = jnp.concatenate([piece[:, :width] for piece in pieces], axis=0)
    table = jnp.concatenate([piece[:, width:] for piece in pieces], axis=0).astype(f32)
    lane = lax.broadcasted_iota(jnp.int32, table.shape, 1)
    place = lax.axis_index("ep")
    partner = place + 1 - 2 * (place % 2)
    downs = []
    for side, owner in enumerate((place, partner)):
        w_gate, w_up, w_down = sides[3 * side : 3 * side + 3]
        for local in range(local_count):
            expert = owner * local_count + local
            mine = (
                (lane == expert) | (lane == expert + experts) | (lane == expert + 2 * experts)
            )
            slot = len(downs)
            weight[slot] = jnp.broadcast_to(
                jnp.sum(jnp.where(mine, table, 0.0), axis=1, keepdims=True), table.shape
            )
            for f in range(0, hidden, TILE):
                cols = slice(f, f + TILE)
                gate_part = jnp.dot(x, w_gate[local, :, cols], preferred_element_type=f32)
                up_part = jnp.dot(x, w_up[local, :, cols], preferred_element_type=f32)
                silu = gate_part / (1.0 + jnp.exp(-gate_part))
                inner[slot, :, cols] = (silu * up_part).astype(jnp.bfloat16)
            downs.append((w_down, local))
    for d in range(0, width, TILE):
        totals = [0.0] * (TILE // LANES)
        for slot, (w_down, local) in enumerate(downs):
            out = jnp.dot(inner[slot], w_down[local, :, d : d + TILE], preferred_element_type=f32)
            out = out.astype(jnp.bfloat16).astype(f32)
            for j in range(TILE // LANES):
                totals[j] = totals[j] + out[:, j * LANES : (j + 1) * LANES] * weight[slot]
        for j, total in enumerate(totals):
            cols = slice(d + j * LANES, d + (j + 1) * LANES)
            first = 0
            for result in outs:
                last = first + result.shape[0]
                result[:, cols] = total[first:last].astype(result.dtype)
                first = last


def expert_rows(pieces, weights, experts, outs):
    rows = sum(piece.shape[0] for piece in pieces)
    local_count, width, hidden = weights[0].shape
    count = len(pieces)
    vmem = pl.BlockSpec(memory_space=pltpu.VMEM)
    return pl.pallas_call(
        functools.partial(
            expert_body, count=count, experts=experts, local_count=local_count
        ),
        out_shape=tuple(jax.ShapeDtypeStruct((n, width), kind) for n, kind in outs),
        in_specs=[vmem] * (count + 6),
        out_specs=(vmem,) * len(outs),
        scratch_shapes=[
            pltpu.VMEM((2 * local_count, rows, hidden), jnp.bfloat16),
            pltpu.VMEM((2 * local_count, rows, LANES), jnp.float32),
        ],
        compiler_params=pltpu.CompilerParams(vmem_limit_bytes=16 * MIB),
        cost_estimate=pl.CostEstimate(
            flops=12 * rows * width * hidden * local_count,
            bytes_accessed=12 * width * hidden * local_count,
            transcendentals=2 * rows * hidden,
        ),
        name="expert_rows",
    )(*pieces, *weights)


def level_body(own, *refs, first):
    total = own[...]
    for ref in refs[:-1]:
        total = total + ref[first : first + own.shape[0]].astype(jnp.float32)
    refs[-1][...] = total.astype(jnp.bfloat16)


def level_sum(own, arrived, first=0):
    vmem = pl.BlockSpec(memory_space=pltpu.VMEM)
    return pl.pallas_call(
        functools.partial(level_body, first=first),
        out_shape=jax.ShapeDtypeStruct(own.shape, jnp.bfloat16),
        in_specs=[vmem] * (1 + len(arrived)),
        out_specs=vmem,
        compiler_params=pltpu.CompilerParams(vmem_limit_bytes=4 * MIB),
        name="level_sum",
    )(own, *arrived)


def dense(payload, resid, weights):
    devices = lax.axis_size("ep")
    experts = devices * weights[0].shape[0]
    zs, ys, _ = grid_of(devices)
    dys = range(1, ys)
    f32 = jnp.float32
    rows = payload.shape[0]
    pieces = gathered(payload)
    total = resid
    sums = {}
    for number, dz in enumerate(far_levels(zs)):
        level = (1, 0)[number]
        places = [(dz, dy) for dy in range(ys)] + [(level, dy) for dy in range(ys)]
        outs = {place: (rows, jnp.bfloat16 if place in places[1:ys] else f32) for place in places}
        if level:
            outs = {place: outs[place] for place in places[:ys]}
            outs["side"] = (ys * rows, jnp.bfloat16)
        results = expert_rows(
            [pieces[place] for place in places], weights, experts, list(outs.values())
        )
        sums.update(zip(outs, results))
        arrived = [send(sums[dz, dy], 0, dy, 0) for dy in dys]
        level = level_sum(sums[dz, 0], arrived)
        total = total + send(level, dz, 0, 0).astype(f32)
    side = send(sums["side"], 1, 0, 0)
    total = total + (sums[0, 0] + side[:rows].astype(f32))
    for dy in dys:
        level = level_sum(sums[0, dy], [side], dy * rows)
        total = total + send(level, 0, dy, 0).astype(f32)
    return total.astype(jnp.bfloat16)


def layer_rows(
    hidden_in,
    queries,
    stored_keys,
    stored_values,
    stored_lengths,
    norm_gain,
    expert_ids,
    gate_weights,
    w_gate,
    w_up,
    w_down,
    capacity,
):
    devices = lax.axis_size("ep")
    experts = devices * w_gate.shape[0]
    if 2 * expert_ids.shape[1] >= experts and dense_fits(devices) and 3 * experts <= LANES:
        other = [send(w, 0, 0, 1) for w in (w_gate, w_up, w_down)]
        payload, resid, w_gate = attention(
            hidden_in, queries, stored_keys, stored_values, stored_lengths, norm_gain,
            expert_ids, gate_weights, w_gate, experts,
        )
        w_down = loaded(payload, w_down)
        w_up = loaded(payload, w_up)
        return dense(payload, resid, (w_gate, w_up, w_down, *other))
    attention_output = cached_attention(
        queries, stored_keys, stored_values, stored_lengths, QUERY_HEADS, KEY_VALUE_HEADS
    )
    resid = hidden_in.astype(jnp.float32) + attention_output
    mean_square = jnp.mean(resid * resid, axis=-1, keepdims=True)
    normed = (resid * lax.rsqrt(mean_square + 1e-06) * norm_gain[None, :]).astype(jnp.bfloat16)
    mixture = routed(normed, expert_ids, gate_weights, w_gate, w_up, w_down, capacity)
    return (resid + mixture).astype(jnp.bfloat16)


def local(
    hidden_in,
    queries,
    stored_keys,
    stored_values,
    stored_lengths,
    norm_gain,
    expert_ids,
    gate_weights,
    w_gate,
    w_up,
    w_down,
):
    experts = lax.axis_size("ep") * w_gate.shape[0]
    top_count = expert_ids.shape[1]
    capacity = max(2, 3 * MB_ROWS * top_count // (2 * experts))
    return layer_rows(
        hidden_in,
        queries,
        stored_keys,
        stored_values,
        stored_lengths,
        norm_gain,
        expert_ids,
        gate_weights,
        w_gate,
        w_up,
        w_down,
        MB * capacity,
    )


def solution(mesh):
    in_specs = (
        P(("groups", "ep"), None),
        P(("groups", "ep"), None),
        P(("groups", "ep"), None, None),
        P(("groups", "ep"), None, None),
        P(("groups", "ep")),
        P(),
        P(("groups", "ep"), None),
        P(("groups", "ep"), None),
        P("ep", None, None),
        P("ep", None, None),
        P("ep", None, None),
    )
    out_specs = P(("groups", "ep"), None)
    step = jax.shard_map(local, mesh=mesh, in_specs=in_specs, out_specs=out_specs, check_vma=False)
    if not dense_fits(mesh.shape["ep"]):
        return step
    return step
```
